128 devices in a mesh: dp: 4 (over y_lo, core), context: 32 (over y_hi, x, z).
Axes of the slice: x: 4, y: 4 (y_hi: 2, y_lo: 2; y = y_hi * 2 + y_lo), z: 4, core: 2. Of those that a mesh axis runs over, the one named last changes fastest.
Arguments:
- query_in: bfloat16 [4, 4096, 8192], P('dp', 'context'), may hold values from -6 to 6
- key_in: bfloat16 [4, 4096, 8192], P('dp', 'context'), may hold values from -6 to 6
- value_in: bfloat16 [4, 4096, 8192], P('dp', 'context'), may hold values from -6 to 6
- grad_out: bfloat16 [4, 4096, 8192], P('dp', 'context'), may hold values from -6 to 6
- med_filter: float32 [8192, 128], P('context', 'dp'), may hold values from -0.5 to 0.5
- short_filter: float32 [3, 8192, 7], P(None, 'context'), may hold values from -2 to 2
Outputs:
- mixed: bfloat16 [4, 4096, 8192], P('dp', 'context')
- grad_q: bfloat16 [4, 4096, 8192], P('dp', 'context')
- grad_k: bfloat16 [4, 4096, 8192], P('dp', 'context')
- grad_v: bfloat16 [4, 4096, 8192], P('dp', 'context')
- grad_med: float32 [8192, 128], P('context', 'dp')
- grad_short: float32 [3, 8192, 7], P(None, 'context')
The draws below stay inside these ranges and needn't reach their ends.
All inputs are finite; a program needn't handle non-finite values.
Results may differ from the reference program's by a relative error of at most 0.0058.
Values may be sent and summed in bfloat16 or wider, within the bound.
No kernel may reach another device: no remote copies, remote signals or barrier semaphores. Data moves between devices by JAX's collectives and lax.ppermute only.
A program may use at most 256 MiB of HBM per device.

```python
import jax
import jax.numpy as jnp
from jax import lax

D = 8192
MED = 128
SHORT = 7
LEN = 4096
SEQS = 4
N_CONTEXT = 32


def steps_of(stream_key, shape, cuts, least, top_value):
    def one(position, shards_of):
        steps = jax.random.uniform(jax.random.fold_in(jax.random.fold_in(stream_key, 6), position), (shards_of,), jnp.float32, least / len(cuts), top_value / len(cuts))
        return jnp.repeat(jnp.exp(steps), shape[position] // shards_of).reshape((-1,) + (1,) * (len(shape) - position - 1))

    factor_of = one(*cuts[0])
    for cut in cuts[1:]:
        factor_of = factor_of * one(*cut)
    return factor_of


def normal_values(rng, dims, deviation, reach, pieces=(), held_as=jnp.bfloat16):
    values = deviation * jax.random.normal(rng, dims, jnp.float32)
    if pieces:
        values = values * steps_of(rng, dims, pieces, -0.22, 0.18)
    return jnp.clip(values, -reach, reach).astype(held_as)


def setup_inputs(seed: int = 0) -> dict:
    splits = jax.random.split(jax.random.key(seed), 7)
    return {
        "query_in": normal_values(splits[0], (SEQS, LEN, D), 1.0, 6.0, ((0, 4), (1, 32))),
        "key_in": normal_values(splits[1], (SEQS, LEN, D), 1.0, 6.0, ((0, 4), (1, 32))),
        "value_in": normal_values(splits[2], (SEQS, LEN, D), 1.0, 6.0, ((0, 4), (1, 32))),
        "grad_out": normal_values(splits[3], (SEQS, LEN, D), 1.0, 6.0, ((0, 4), (1, 32))),
        "med_filter": normal_values(splits[4], (D, MED), MED ** -0.5, 0.5, ((0, 32), (1, 4)), jnp.float32),
        "short_filter": normal_values(splits[5], (3, D, SHORT), SHORT ** -0.5, 2.0, ((1, 32),), jnp.float32),
    }


def short_forward(rows, before, taps):
    width = taps.shape[1]
    count = rows.shape[0]
    padded = jnp.concatenate([before, rows], axis=0).astype(jnp.float32)
    total = jnp.zeros(rows.shape, jnp.float32)
    for offset in range(width):
        start = width - 1 - offset
        total = total + taps[:, offset] * padded[start:start + count]
    return total


def short_backward(grads, after, taps):
    width = taps.shape[1]
    count = grads.shape[0]
    padded = jnp.concatenate([grads, after], axis=0)
    total = jnp.zeros(grads.shape, jnp.float32)
    for offset in range(width):
        total = total + taps[:, offset] * padded[offset:offset + count]
    return total


def short_weight(grads, rows, before):
    width = before.shape[0] + 1
    count = rows.shape[0]
    padded = jnp.concatenate([before, rows], axis=0).astype(jnp.float32)
    columns = []
    for offset in range(width):
        start = width - 1 - offset
        columns.append(jnp.sum(grads * padded[start:start + count], axis=0))
    return jnp.stack(columns, axis=1)


def toeplitz(taps):
    size = taps.shape[1]
    index = lax.broadcasted_iota(jnp.int32, (size, 2 * size), 0) + size - lax.broadcasted_iota(jnp.int32, (size, 2 * size), 1)
    valid = (index >= 0) & (index < size)
    picked = taps[:, jnp.clip(index, 0, size - 1)]
    return jnp.where(valid[None], picked, jnp.zeros((), taps.dtype))


def windows(rows, before):
    size = before.shape[0] + 1
    first = jnp.concatenate([jnp.zeros((1, rows.shape[1]), rows.dtype), before], axis=0)
    blocks = rows.reshape(rows.shape[0] // size, size, rows.shape[1])
    earlier = jnp.concatenate([first[None], blocks[:-1]], axis=0)
    return jnp.concatenate([earlier, blocks], axis=1)


def medium_conv(rows, before, toep):
    frames = windows(rows, before).astype(jnp.float32)
    out = jnp.einsum("brc,csr->bsc", frames, toep.astype(jnp.float32))
    return out.reshape(rows.shape)


def medium_weight(grads, rows, before):
    size = before.shape[0] + 1
    frames = windows(rows, before).astype(jnp.float32)
    blocks = grads.reshape(-1, size, grads.shape[1]).astype(jnp.float32)
    outer = jnp.einsum("bsc,brc->csr", blocks, frames)
    chans = outer.shape[0]
    padded = jnp.pad(outer, ((0, 0), (0, 0), (0, 1)))
    flat = padded.reshape(chans, size * (2 * size + 1))
    flat = jnp.pad(flat, ((0, 0), (0, size)))
    sheared = flat.reshape(chans, size, 2 * size + 2)
    return jnp.flip(jnp.sum(sheared[:, :, 1:size + 1], axis=1), axis=1)


def one_sequence(query, keys, values, cotangent, toep, shorts):
    chans = query.shape[1]
    rim_short = jnp.zeros((shorts.shape[2] - 1, chans), jnp.bfloat16)
    rim_med = jnp.zeros((toep.shape[1] - 1, chans), jnp.bfloat16)
    after_short = jnp.zeros((shorts.shape[2] - 1, chans), jnp.float32)
    q_short = short_forward(query, rim_short, shorts[0])
    k_short = short_forward(keys, rim_short, shorts[1])
    v_short = short_forward(values, rim_short, shorts[2])
    product = (k_short * v_short).astype(jnp.bfloat16)
    conv_out = medium_conv(product, rim_med, toep)
    mixed = (q_short * conv_out).astype(jnp.bfloat16)
    grad_f = cotangent.astype(jnp.float32)
    grad_z = (grad_f * q_short).astype(jnp.bfloat16)
    grad_qs = grad_f * conv_out
    grad_u = jnp.flip(medium_conv(jnp.flip(grad_z, 0), rim_med, toep), 0)
    grad_ks = grad_u * v_short
    grad_vs = grad_u * k_short
    grad_q = short_backward(grad_qs, after_short, shorts[0]).astype(jnp.bfloat16)
    grad_k = short_backward(grad_ks, after_short, shorts[1]).astype(jnp.bfloat16)
    grad_v = short_backward(grad_vs, after_short, shorts[2]).astype(jnp.bfloat16)
    grad_med = medium_weight(grad_z, product, rim_med)
    grad_short = jnp.stack([short_weight(grad_qs, query, rim_short), short_weight(grad_ks, keys, rim_short), short_weight(grad_vs, values, rim_short)], axis=0)
    return mixed, grad_q, grad_k, grad_v, grad_med, grad_short


def reference(query_in, key_in, value_in, grad_out, med_filter, short_filter):
    seqs, length, width = query_in.shape
    count = N_CONTEXT
    group = width // count

    def split(x):
        return x.reshape(seqs, length, count, group).transpose(2, 0, 1, 3)

    taps = med_filter.astype(jnp.bfloat16).reshape(count, group, -1)
    shorts = short_filter.reshape(3, count, group, -1).transpose(1, 0, 2, 3)

    def block(items):
        query, keys, values, cotangent, htaps, stap = items
        toep = toeplitz(htaps)
        outs = jax.vmap(lambda a, b, c, d: one_sequence(a, b, c, d, toep, stap))(query, keys, values, cotangent)
        return outs[0], outs[1], outs[2], outs[3], jnp.sum(outs[4], axis=0), jnp.sum(outs[5], axis=0)

    result = lax.map(block, (split(query_in), split(key_in), split(value_in), split(grad_out), taps, shorts))

    def merge(x):
        return x.transpose(1, 2, 0, 3).reshape(seqs, length, width)

    grad_med = result[4].reshape(width, -1)
    grad_short = result[5].transpose(1, 0, 2, 3).reshape(3, width, -1)
    return (merge(result[0]), merge(result[1]), merge(result[2]), merge(result[3]), grad_med, grad_short)
```

```python
import functools

import jax
import jax.numpy as jnp
import numpy as np
from jax import lax
from jax.experimental import pallas as pl
from jax.experimental.pallas import tpu as pltpu
from jax.sharding import PartitionSpec as P

BF = jnp.bfloat16
F32 = jnp.float32
LANES = 128
ROW = 8


def phases(tokens, size):
    angle = 2.0 * np.pi * (np.arange(size // 2)[:, None] + 0.5) * tokens[None, :] / size
    return np.concatenate([np.cos(angle), np.sin(angle)], axis=0)


def split_host(table):
    high = table.astype(BF)
    low = (table - high.astype(np.float64)).astype(BF)
    return jnp.asarray(high), jnp.asarray(low)


def transforms(block, width):
    size = 2 * block
    reach = width - 1
    own = np.arange(block)
    behind = np.where(own < reach, own + block, own - block)
    ahead = own + block
    rows = np.arange(block + ROW)
    forward = [
        split_host(phases(np.concatenate([own, behind]), size)),
        split_host(phases(own, size)),
        split_host(phases(ahead, size)),
    ]
    inverse = split_host(phases(rows, size).T * (2.0 / size))
    return forward, inverse


def split_bf(x):
    high = x.astype(BF)
    low = (x - high.astype(F32)).astype(BF)
    return high, low


def dot(a, b):
    return jnp.dot(a, b, preferred_element_type=F32)


def row_of(ref, index, lanes):
    return ref[pl.ds(index, 1), lanes]


def load_padded(dst, own_ref, before, after, lanes, block):
    dst[pl.ds(0, ROW), :] = before
    dst[pl.ds(ROW, block), :] = own_ref[0, :, lanes].astype(F32)
    dst[pl.ds(ROW + block, ROW), :] = after


def causal(src, taps, first, width, lanes, rows):
    total = None
    for offset in range(width):
        term = row_of(taps, first + offset, lanes) * src[pl.ds(ROW - offset, rows), :]
        total = term if total is None else total + term
    return total


def make_products(block, width, cols, q, k, v, go, back, fore, taps, u_out, dz_out, x_q, x_k, x_v):
    for col in range(cols):
        lanes = pl.ds(col * LANES, LANES)
        for which, (src, dst) in enumerate(((q, x_q), (k, x_k), (v, x_v))):
            load_padded(
                dst.at[col],
                src,
                back[which, :, lanes].astype(F32),
                fore[which, :, lanes].astype(F32),
                lanes,
                block,
            )
        k_s = causal(x_k.at[col], taps, width, width, lanes, block)
        v_s = causal(x_v.at[col], taps, 2 * width, width, lanes, block)
        u_out[:, lanes] = (k_s * v_s).astype(BF)
        q_s = causal(x_q.at[col], taps, 0, width, lanes, block + ROW)
        dz_out[0:block, lanes] = (go[0, :, lanes].astype(F32) * q_s[0:block]).astype(BF)
        dz_out[block : block + ROW, lanes] = (
            fore[3, :, lanes].astype(F32) * q_s[block : block + ROW]
        ).astype(BF)


def mixer(
    block,
    width,
    cols,
    q,
    k,
    v,
    go,
    back,
    fore,
    taps,
    u_prev,
    dz_next,
    h_ref,
    fx_hi,
    fx_lo,
    fo_hi,
    fo_lo,
    fa_hi,
    fa_lo,
    in_hi,
    in_lo,
    mixed,
    g_q,
    g_k,
    g_v,
    g_med,
    g_short,
    x_q,
    x_k,
    x_v,
    s_q,
    s_k,
    s_v,
    g_pad,
    h_pad,
    h_flip,
    z_pad,
    window,
    dz_own,
    edge_u,
    edge_z,
    spec_u,
    spec_h,
    spec_d,
    spec_w,
    prod_hi,
    prod_lo,
):
    rows = block + ROW
    half = block
    rank = lax.broadcasted_iota(jnp.int32, (ROW, LANES), 0)
    for col in range(cols):
        lanes = pl.ds(col * LANES, LANES)
        for which, (src, dst) in enumerate(((q, x_q), (k, x_k), (v, x_v))):
            load_padded(
                dst.at[col],
                src,
                back[which, :, lanes].astype(F32),
                fore[which, :, lanes].astype(F32),
                lanes,
                block,
            )
        q_s = causal(x_q.at[col], taps, 0, width, lanes, rows)
        s_q[col] = q_s
        dz = (go[0, :, lanes].astype(F32) * q_s[0:block]).astype(BF)
        dz_own[:, lanes] = dz
        z_pad[col, 0:ROW, :] = jnp.zeros((ROW, LANES), F32)
        z_pad[col, ROW : 2 * ROW, :] = dz[0:ROW].astype(F32)
        k_s = causal(x_k.at[col], taps, width, width, lanes, rows)
        s_k[col] = k_s
        v_s = causal(x_v.at[col], taps, 2 * width, width, lanes, rows)
        s_v[col] = v_s
        u = (k_s * v_s).astype(BF)
        window[0:block, lanes] = u[0:block]
        u_after = u[block:rows].astype(F32)
        first = u_prev[0 : 2 * ROW, lanes]
        u_before = first.astype(F32)[0:ROW]
        patched = jnp.where(rank < width - 1, u_after, u_before)
        window[block : block + 2 * ROW, lanes] = jnp.concatenate(
            [patched, first.astype(F32)[ROW : 2 * ROW]], axis=0
        ).astype(BF)
        window[block + 2 * ROW : 2 * block, lanes] = u_prev[2 * ROW : block, lanes]
        edge_u[col] = u_before + u_after
        edge_z[col] = dz_next[block : block + ROW, lanes].astype(F32) + dz[0:ROW].astype(F32)
        taps_h = h_ref[0, :, lanes].astype(F32)
        h_pad[col, 0 : 2 * ROW, :] = taps_h[block - 2 * ROW : block]
        h_pad[col, 2 * ROW : 3 * ROW, :] = jnp.zeros((ROW, LANES), F32)
        h_flip[col, 0:ROW, :] = jnp.zeros((ROW, LANES), F32)
        for place in range(ROW):
            h_flip[col, ROW + place : ROW + place + 1, :] = h_pad[
                col, 2 * ROW - 1 - place : 2 * ROW - place, :
            ]

    x = window[...]
    spec_u[...] = dot(fx_hi[...], x) + dot(fx_lo[...], x)
    h = h_ref[0]
    spec_h[...] = dot(fo_hi[...], h) + dot(fo_lo[...], h)
    d = dz_own[...]
    spec_d[...] = dot(fo_hi[...], d) + dot(fo_lo[...], d)
    a = dz_next[0:block, :]
    spec_w[...] = spec_d[...] + (dot(fa_hi[...], a) + dot(fa_lo[...], a))

    def inverse(slot, count):
        high, low = prod_hi[slot], prod_lo[slot]
        top, rest = in_hi[0:count, :], in_lo[0:count, :]
        return dot(top, high) + (dot(rest, high) + dot(top, low))

    def store(slot, cos_part, sin_part):
        for place, part in ((0, cos_part), (half, sin_part)):
            high, low = split_bf(part)
            prod_hi[slot, place : place + half, :] = high
            prod_lo[slot, place : place + half, :] = low

    uc, us = spec_u[0:half, :], spec_u[half:, :]
    hc, hs = spec_h[0:half, :], spec_h[half:, :]
    store(0, uc * hc - us * hs, uc * hs + us * hc)
    wc, ws = spec_w[0:half, :], spec_w[half:, :]
    store(1, wc * hc + ws * hs, ws * hc - wc * hs)
    dc, ds = spec_d[0:half, :], spec_d[half:, :]
    store(2, dc * uc + ds * us, ds * uc - dc * us)

    z_all = inverse(0, rows)
    du_all = inverse(1, rows)
    gm_all = inverse(2, block)

    for col in range(cols):
        lanes = pl.ds(col * LANES, LANES)
        lo, hi = col * LANES, (col + 1) * LANES
        z = z_all[:, lo:hi]
        du = du_all[:, lo:hi]
        gm = gm_all[:, lo:hi]
        z_fix = jnp.zeros((ROW, LANES), F32)
        g_fix = jnp.zeros((ROW, LANES), F32)
        for place in range(1, width - 1):
            held = edge_u[col, place : place + 1, :]
            z_fix = z_fix + held * h_pad[col, pl.ds(2 * ROW - place, ROW), :]
            g_fix = g_fix + held * z_pad[col, pl.ds(place, ROW), :]
        du_fix = jnp.zeros((ROW, LANES), F32)
        for place in range(width - 2):
            held = edge_z[col, place : place + 1, :]
            du_fix = du_fix + held * h_flip[col, pl.ds(ROW - 1 - place, ROW), :]
        z = jnp.concatenate([z[0:ROW] + z_fix, z[ROW:]], axis=0)
        du = jnp.concatenate([du[0:block], du[block:] + du_fix], axis=0)
        g_med[0, 0 : block - ROW, lanes] = gm[0 : block - ROW]
        g_med[0, block - ROW : block, lanes] = gm[block - ROW : block] + g_fix
        mixed[0, :, lanes] = (s_q[col, 0:block, :] * z[0:block]).astype(BF)
        g_pad[0, 0:block, :] = go[0, :, lanes].astype(F32) * z[0:block]
        g_pad[0, block:rows, :] = fore[3, :, lanes].astype(F32) * z[block:rows]
        g_pad[1] = du * s_v[col]
        g_pad[2] = du * s_k[col]
        for which, (src, out) in enumerate(((x_q, g_q), (x_k, g_k), (x_v, g_v))):
            values = src[col, ROW : ROW + block, :]
            total = None
            for offset in range(width):
                moved = g_pad[which, pl.ds(offset, block), :]
                term = row_of(taps, which * width + offset, lanes) * moved
                total = term if total is None else total + term
                g_short[0, which * width + offset : which * width + offset + 1, lanes] = jnp.sum(
                    values * moved, axis=0, keepdims=True
                )
            out[0, :, lanes] = total.astype(BF)


def halo_pairs(count):
    return [(i, i + 1) for i in range(count - 1)], [(i + 1, i) for i in range(count - 1)]


def per_device(n_context, n_dp, query_in, key_in, value_in, grad_out, med_filter, short_filter):
    _, block, width_all = query_in.shape
    group, taps_own = med_filter.shape
    width = short_filter.shape[2]
    size = 2 * block
    ahead, behind = halo_pairs(n_context)
    forward, inverse = transforms(block, width)

    back = jnp.concatenate([x[:, block - ROW :] for x in (query_in, key_in, value_in)], axis=0)
    fore = jnp.concatenate([x[:, :ROW] for x in (query_in, key_in, value_in, grad_out)], axis=0)
    back = lax.ppermute(back, "context", ahead)
    fore = lax.ppermute(fore, "context", behind)

    h_all, taps = share_filters(med_filter, short_filter)

    tile = 4 * LANES
    cols = tile // LANES
    tokens = pl.BlockSpec((1, block, tile), lambda i: (0, 0, i))
    flat = lambda height: pl.BlockSpec((height, tile), lambda i: (0, i))
    stack = lambda count: pl.BlockSpec((count, ROW, tile), lambda i: (0, 0, i))
    padded = pltpu.VMEM((cols, block + 2 * ROW, LANES), F32)
    u, dz = pl.pallas_call(
        functools.partial(make_products, block, width, cols),
        grid=(width_all // tile,),
        in_specs=[tokens] * 4 + [stack(3), stack(4), flat(taps.shape[0])],
        out_specs=[flat(block), flat(block + ROW)],
        out_shape=[
            jax.ShapeDtypeStruct((block, width_all), BF),
            jax.ShapeDtypeStruct((block + ROW, width_all), BF),
        ],
        scratch_shapes=[padded] * 3,
        name="products",
    )(query_in, key_in, value_in, grad_out, back, fore, taps)

    u_prev = lax.ppermute(u, "context", ahead)
    dz_next = lax.ppermute(dz, "context", behind)

    tile = group
    cols = tile // LANES
    tokens = pl.BlockSpec((1, block, tile), lambda i: (0, 0, i))
    flat = lambda height: pl.BlockSpec((height, tile), lambda i: (0, i))
    stack = lambda count: pl.BlockSpec((count, ROW, tile), lambda i: (0, 0, i))
    whole = lambda x: pl.BlockSpec(x.shape, lambda i: (0,) * x.ndim)
    per_group = lambda height: pl.BlockSpec((1, height, tile), lambda i: (i, 0, 0))
    tables = [part for pair in forward + [inverse] for part in pair]
    padded = pltpu.VMEM((cols, block + 2 * ROW, LANES), F32)
    shifted = pltpu.VMEM((cols, block + ROW, LANES), F32)
    held_short = 3 * ROW
    mixed, grad_q, grad_k, grad_v, part_med, part_short = pl.pallas_call(
        functools.partial(mixer, block, width, cols),
        grid=(width_all // tile,),
        in_specs=[tokens] * 4
        + [stack(3), stack(4), flat(taps.shape[0]), flat(block), flat(block + ROW), per_group(block)]
        + [whole(x) for x in tables],
        out_specs=[tokens] * 4 + [per_group(block), per_group(held_short)],
        out_shape=[jax.ShapeDtypeStruct(query_in.shape, BF)] * 4
        + [
            jax.ShapeDtypeStruct((n_context, block, group), F32),
            jax.ShapeDtypeStruct((n_context, held_short, group), F32),
        ],
        scratch_shapes=[
            padded,
            padded,
            padded,
            shifted,
            shifted,
            shifted,
            pltpu.VMEM((3, block + ROW, LANES), F32),
            pltpu.VMEM((cols, 3 * ROW, LANES), F32),
            pltpu.VMEM((cols, 2 * ROW, LANES), F32),
            pltpu.VMEM((cols, 2 * ROW, LANES), F32),
            pltpu.VMEM((size, tile), BF),
            pltpu.VMEM((block, tile), BF),
            pltpu.VMEM((cols, ROW, LANES), F32),
            pltpu.VMEM((cols, ROW, LANES), F32),
            pltpu.VMEM((size, tile), F32),
            pltpu.VMEM((size, tile), F32),
            pltpu.VMEM((size, tile), F32),
            pltpu.VMEM((size, tile), F32),
            pltpu.VMEM((3, size, tile), BF),
            pltpu.VMEM((3, size, tile), BF),
        ],
        name="mixer",
    )(
        query_in,
        key_in,
        value_in,
        grad_out,
        back,
        fore,
        taps,
        u_prev,
        dz_next,
        h_all,
        *tables,
    )

    grad_med, grad_short = reduce_filters(part_med, part_short, n_dp, width, taps_own)
    return (mixed, grad_q, grad_k, grad_v, grad_med, grad_short)


def share_filters(med_filter, short_filter):
    mine = med_filter.astype(BF).T
    column = lax.all_gather(mine, "dp", axis=0, tiled=True)
    n = lax.axis_size("context")
    h_all = lax.all_to_all(jnp.broadcast_to(column, (n,) + column.shape), "context", 0, 0)
    short = short_filter.transpose(0, 2, 1).reshape(-1, short_filter.shape[1])
    short = jnp.pad(short, ((0, -short.shape[0] % ROW), (0, 0)))
    taps = lax.all_to_all(jnp.broadcast_to(short, (n,) + short.shape), "context", 0, 0)
    return h_all, taps.transpose(1, 0, 2).reshape(short.shape[0], -1)


def reduce_filters(part_med, part_short, n_dp, width, taps_own):
    med = jnp.sum(lax.all_to_all(part_med, "context", 0, 0), axis=0)
    med = lax.psum_scatter(med, "dp", scatter_dimension=0, tiled=True)
    short = jnp.sum(lax.all_to_all(part_short, "context", 0, 0), axis=0)
    short = lax.psum(short, "dp")
    group = short.shape[1]
    return med.T, short[: 3 * width].reshape(3, width, group).transpose(0, 2, 1)


def solution(mesh):
    tokens = P("dp", "context", None)
    filters = (P("context", "dp"), P(None, "context", None))
    return jax.shard_map(
        functools.partial(per_device, mesh.shape["context"], mesh.shape["dp"]),
        mesh=mesh,
        in_specs=(tokens,) * 4 + filters,
        out_specs=(tokens,) * 4 + filters,
        check_vma=False,
    )
```

```python
import functools

import jax
import jax.numpy as jnp
import numpy as np
from jax import lax
from jax.experimental import pallas as pl
from jax.experimental.pallas import tpu as pltpu
from jax.sharding import PartitionSpec as P


PARTS = 4
BF = jnp.bfloat16
F32 = jnp.float32
LANES = 128
ROW = 8


def phases(tokens, size):
    angle = 2.0 * np.pi * (np.arange(size // 2)[:, None] + 0.5) * tokens[None, :] / size
    return np.concatenate([np.cos(angle), np.sin(angle)], axis=0)


def split_host(table):
    high = table.astype(BF)
    low = (table - high.astype(np.float64)).astype(BF)
    return jnp.asarray(high), jnp.asarray(low)


def transforms(block, width):
    size = 2 * block
    reach = width - 1
    own = np.arange(block)
    behind = np.where(own < reach, own + block, own - block)
    ahead = own + block
    rows = np.arange(block + ROW)
    forward = [
        split_host(phases(np.concatenate([own, behind]), size)),
        split_host(phases(own, size)),
        split_host(phases(ahead, size)),
    ]
    inverse = split_host(phases(rows, size).T * (2.0 / size))
    return forward, inverse


def split_bf(x):
    high = x.astype(BF)
    low = (x - high.astype(F32)).astype(BF)
    return high, low


def dot(a, b):
    return jnp.dot(a, b, preferred_element_type=F32)


def row_of(ref, index, lanes):
    return ref[0, pl.ds(index, 1), lanes]


def load_padded(dst, own_ref, before, after, lanes, block):
    dst[pl.ds(0, ROW), :] = before
    dst[pl.ds(ROW, block), :] = own_ref[0, :, lanes].astype(F32)
    dst[pl.ds(ROW + block, ROW), :] = after


def causal(src, taps, first, width, lanes, rows):
    total = None
    for offset in range(width):
        term = row_of(taps, first + offset, lanes) * src[pl.ds(ROW - offset, rows), :]
        total = term if total is None else total + term
    return total


def make_products(block, width, cols, q, k, v, go, back, fore, taps, u_out, dz_out, x_q, x_k, x_v):
    for col in range(cols):
        lanes = pl.ds(col * LANES, LANES)
        for which, (src, dst) in enumerate(((q, x_q), (k, x_k), (v, x_v))):
            load_padded(
                dst.at[col],
                src,
                back[which, :, lanes].astype(F32),
                fore[which, :, lanes].astype(F32),
                lanes,
                block,
            )
        k_s = causal(x_k.at[col], taps, width, width, lanes, block)
        v_s = causal(x_v.at[col], taps, 2 * width, width, lanes, block)
        u_out[:, lanes] = (k_s * v_s).astype(BF)
        q_s = causal(x_q.at[col], taps, 0, width, lanes, block + ROW)
        dz_out[0:block, lanes] = (go[0, :, lanes].astype(F32) * q_s[0:block]).astype(BF)
        dz_out[block : block + ROW, lanes] = (
            fore[3, :, lanes].astype(F32) * q_s[block : block + ROW]
        ).astype(BF)


def mixer(
    block,
    width,
    cols,
    q,
    k,
    v,
    go,
    back,
    fore,
    taps,
    u_prev,
    dz_next,
    h_ref,
    fx_hi,
    fx_lo,
    fo_hi,
    fo_lo,
    fa_hi,
    fa_lo,
    in_hi,
    in_lo,
    *rest,
):
    rest = rest[len(rest) - 26 :]
    (
    mixed,
    g_q,
    g_k,
    g_v,
    g_part,
    sums,
    x_q,
    x_k,
    x_v,
    s_q,
    s_k,
    s_v,
    g_pad,
    h_pad,
    h_flip,
    z_pad,
    window,
    dz_own,
    edge_u,
    edge_z,
    spec_u,
    spec_h,
    spec_d,
    spec_w,
    prod_hi,
    prod_lo,
    ) = rest
    rows = block + ROW
    half = block
    rank = lax.broadcasted_iota(jnp.int32, (ROW, LANES), 0)
    for col in range(cols):
        lanes = pl.ds(col * LANES, LANES)
        for which, (src, dst) in enumerate(((q, x_q), (k, x_k), (v, x_v))):
            load_padded(
                dst.at[col],
                src,
                back[which, :, lanes].astype(F32),
                fore[which, :, lanes].astype(F32),
                lanes,
                block,
            )
        q_s = causal(x_q.at[col], taps, 0, width, lanes, rows)
        s_q[col] = q_s
        dz = (go[0, :, lanes].astype(F32) * q_s[0:block]).astype(BF)
        dz_own[:, lanes] = dz
        z_pad[col, 0:ROW, :] = jnp.zeros((ROW, LANES), F32)
        z_pad[col, ROW : 2 * ROW, :] = dz[0:ROW].astype(F32)
        k_s = causal(x_k.at[col], taps, width, width, lanes, rows)
        s_k[col] = k_s
        v_s = causal(x_v.at[col], taps, 2 * width, width, lanes, rows)
        s_v[col] = v_s
        u = (k_s * v_s).astype(BF)
        window[0:block, lanes] = u[0:block]
        u_after = u[block:rows].astype(F32)
        first = u_prev[0 : 2 * ROW, lanes]
        u_before = first.astype(F32)[0:ROW]
        patched = jnp.where(rank < width - 1, u_after, u_before)
        window[block : block + 2 * ROW, lanes] = jnp.concatenate(
            [patched, first.astype(F32)[ROW : 2 * ROW]], axis=0
        ).astype(BF)
        window[block + 2 * ROW : 2 * block, lanes] = u_prev[2 * ROW : block, lanes]
        edge_u[col] = u_before + u_after
        edge_z[col] = dz_next[block : block + ROW, lanes].astype(F32) + dz[0:ROW].astype(F32)
        taps_h = h_ref[0, :, lanes].astype(F32)
        h_pad[col, 0 : 2 * ROW, :] = taps_h[block - 2 * ROW : block]
        h_pad[col, 2 * ROW : 3 * ROW, :] = jnp.zeros((ROW, LANES), F32)
        h_flip[col, 0:ROW, :] = jnp.zeros((ROW, LANES), F32)
        for place in range(ROW):
            h_flip[col, ROW + place : ROW + place + 1, :] = h_pad[
                col, 2 * ROW - 1 - place : 2 * ROW - place, :
            ]

    x = window[...]
    spec_u[...] = dot(fx_hi[...], x) + dot(fx_lo[...], x)
    h = h_ref[0]
    spec_h[...] = dot(fo_hi[...], h) + dot(fo_lo[...], h)
    d = dz_own[...]
    spec_d[...] = dot(fo_hi[...], d) + dot(fo_lo[...], d)
    a = dz_next[0:block, :]
    spec_w[...] = spec_d[...] + (dot(fa_hi[...], a) + dot(fa_lo[...], a))

    def inverse(slot, count):
        high, low = prod_hi[slot], prod_lo[slot]
        top, rest = in_hi[0:count, :], in_lo[0:count, :]
        return dot(top, high) + (dot(rest, high) + dot(top, low))

    def store(slot, cos_part, sin_part):
        for place, part in ((0, cos_part), (half, sin_part)):
            high, low = split_bf(part)
            prod_hi[slot, place : place + half, :] = high
            prod_lo[slot, place : place + half, :] = low

    uc, us = spec_u[0:half, :], spec_u[half:, :]
    hc, hs = spec_h[0:half, :], spec_h[half:, :]
    store(0, uc * hc - us * hs, uc * hs + us * hc)
    wc, ws = spec_w[0:half, :], spec_w[half:, :]
    store(1, wc * hc + ws * hs, ws * hc - wc * hs)
    dc, ds = spec_d[0:half, :], spec_d[half:, :]
    store(2, dc * uc + ds * us, ds * uc - dc * us)

    z_all = inverse(0, rows)
    du_all = inverse(1, rows)
    gm_all = inverse(2, block)

    for col in range(cols):
        lanes = pl.ds(col * LANES, LANES)
        lo, hi = col * LANES, (col + 1) * LANES
        z = z_all[:, lo:hi]
        du = du_all[:, lo:hi]
        gm = gm_all[:, lo:hi]
        z_fix = jnp.zeros((ROW, LANES), F32)
        g_fix = jnp.zeros((ROW, LANES), F32)
        for place in range(1, width - 1):
            held = edge_u[col, place : place + 1, :]
            z_fix = z_fix + held * h_pad[col, pl.ds(2 * ROW - place, ROW), :]
            g_fix = g_fix + held * z_pad[col, pl.ds(place, ROW), :]
        du_fix = jnp.zeros((ROW, LANES), F32)
        for place in range(width - 2):
            held = edge_z[col, place : place + 1, :]
            du_fix = du_fix + held * h_flip[col, pl.ds(ROW - 1 - place, ROW), :]
        z = jnp.concatenate([z[0:ROW] + z_fix, z[ROW:]], axis=0)
        du = jnp.concatenate([du[0:block], du[block:] + du_fix], axis=0)
        gm = jnp.concatenate([gm[0 : block - ROW], gm[block - ROW : block] + g_fix], axis=0)
        g_part[0, 0:block, lanes] = gm.astype(BF)
        mixed[0, :, lanes] = (s_q[col, 0:block, :] * z[0:block]).astype(BF)
        g_pad[0, 0:block, :] = go[0, :, lanes].astype(F32) * z[0:block]
        g_pad[0, block:rows, :] = fore[3, :, lanes].astype(F32) * z[block:rows]
        g_pad[1] = du * s_v[col]
        g_pad[2] = du * s_k[col]
        for which, (src, out) in enumerate(((x_q, g_q), (x_k, g_k), (x_v, g_v))):
            values = src[col, ROW : ROW + block, :]
            total = None
            for offset in range(width):
                moved = g_pad[which, pl.ds(offset, block), :]
                term = row_of(taps, which * width + offset, lanes) * moved
                total = term if total is None else total + term
                place = which * width + offset
                sums[place : place + 1, :] = jnp.sum(values * moved, axis=0, keepdims=True)
            out[0, :, lanes] = total.astype(BF)
        g_part[0, block : block + 3 * ROW, lanes] = sums[...].astype(BF)


def halo_pairs(count):
    return [(i, i + 1) for i in range(count - 1)], [(i + 1, i) for i in range(count - 1)]


def groups_of(n_context, n_dp, fine):
    coarse = n_context // fine
    inner = [[c * fine + f for f in range(fine)] for c in range(coarse)]
    outer = [[c * fine + f for c in range(coarse)] for f in range(fine)]
    both = [
        [(c * fine + f) * n_dp + d for f in range(fine) for d in range(n_dp)] for c in range(coarse)
    ]
    return inner, outer, both


def exchange(x, axes, groups=None):
    return lax.all_to_all(x, axes, 0, 0, axis_index_groups=groups)


def spread(x, count, axes, groups=None):
    return exchange(jnp.broadcast_to(x, (count,) + x.shape), axes, groups)


def per_device(n_context, n_dp, query_in, key_in, value_in, grad_out, med_filter, short_filter):
    _, block, _ = query_in.shape
    group, taps_own = med_filter.shape
    width = short_filter.shape[2]
    size = 2 * block
    rows = block + ROW
    held_short = 3 * ROW
    parts = PARTS
    coarse = n_context // parts
    ahead, behind = halo_pairs(n_context)
    _, outer, both = groups_of(n_context, n_dp, parts)
    forward, inverse = transforms(block, width)
    tables = [part for pair in forward + [inverse] for part in pair]

    back = jnp.concatenate([x[:, block - ROW :] for x in (query_in, key_in, value_in)], axis=0)
    fore = jnp.concatenate([x[:, :ROW] for x in (query_in, key_in, value_in, grad_out)], axis=0)
    back = lax.ppermute(back, "context", ahead)
    fore = lax.ppermute(fore, "context", behind)

    short = short_filter.transpose(0, 2, 1).reshape(3 * width, group)
    short = jnp.pad(short, ((0, held_short - 3 * width), (0, 0)))
    taps = spread(short, n_context, "context")

    mine = spread(med_filter.astype(BF).T, parts * n_dp, ("context", "dp"), both)
    mine = mine.reshape(parts, block, group)
    h_all = []
    for place in range(2):
        first = place * (parts // 2)
        h_all.append(spread(mine[first : first + parts // 2], coarse, "context", outer))

    cols = group // LANES
    grid = (coarse,)
    padded = pltpu.VMEM((cols, block + 2 * ROW, LANES), F32)
    shifted = pltpu.VMEM((cols, rows, LANES), F32)
    whole = lambda x: pl.BlockSpec(x.shape, lambda i: (0,) * x.ndim)
    packed = lambda height: pl.BlockSpec((height, group), lambda i: (0, i))
    outs = None
    partials = []
    pieces = []
    for part in range(parts):
        tokens = pl.BlockSpec((1, block, group), lambda i, part=part: (0, 0, parts * i + part))
        stack = lambda count, part=part: pl.BlockSpec(
            (count, ROW, group), lambda i: (0, 0, parts * i + part)
        )
        filters = pl.BlockSpec((1, held_short, group), lambda i, part=part: (parts * i + part, 0, 0))
        u, dz = pl.pallas_call(
            functools.partial(make_products, block, width, cols),
            grid=grid,
            in_specs=[tokens] * 4 + [stack(3), stack(4), filters],
            out_specs=[packed(block), packed(rows)],
            out_shape=[
                jax.ShapeDtypeStruct((block, coarse * group), BF),
                jax.ShapeDtypeStruct((rows, coarse * group), BF),
            ],
            scratch_shapes=[padded] * 3,
        )(query_in, key_in, value_in, grad_out, back, fore, taps)
        u_prev = lax.ppermute(u, "context", ahead)
        dz_next = lax.ppermute(dz, "context", behind)
        pieces.append((u_prev, dz_next))
    for part in range(parts):
        tokens = pl.BlockSpec((1, block, group), lambda i, part=part: (0, 0, parts * i + part))
        stack = lambda count, part=part: pl.BlockSpec(
            (count, ROW, group), lambda i: (0, 0, parts * i + part)
        )
        filters = pl.BlockSpec((1, held_short, group), lambda i, part=part: (parts * i + part, 0, 0))
        half = parts // 2
        taps_h = pl.BlockSpec(
            (1, None, block, group), lambda i, part=part: (i, part % half, 0, 0)
        )
        u_prev, dz_next = pieces[part]
        carried = [] if outs is None else list(outs)
        fixed = [query_in, key_in, value_in, grad_out, back, fore, taps, u_prev, dz_next]
        fixed += [h_all[part // half], *tables]
        *outs, partial = pl.pallas_call(
            functools.partial(mixer, block, width, cols),
            grid=grid,
            in_specs=[tokens] * 4
            + [stack(3), stack(4), filters, packed(block), packed(rows), taps_h]
            + [whole(x) for x in tables]
            + [pl.BlockSpec(memory_space=pl.ANY)] * len(carried),
            out_specs=[tokens] * 4
            + [pl.BlockSpec((1, block + held_short, group), lambda i: (i, 0, 0))],
            out_shape=[jax.ShapeDtypeStruct(query_in.shape, BF)] * 4
            + [jax.ShapeDtypeStruct((coarse, block + held_short, group), BF)],
            scratch_shapes=[
                pltpu.VMEM((held_short, LANES), F32),
                padded,
                padded,
                padded,
                shifted,
                shifted,
                shifted,
                pltpu.VMEM((3, rows, LANES), F32),
                pltpu.VMEM((cols, 3 * ROW, LANES), F32),
                pltpu.VMEM((cols, 2 * ROW, LANES), F32),
                pltpu.VMEM((cols, 2 * ROW, LANES), F32),
                pltpu.VMEM((size, group), BF),
                pltpu.VMEM((block, group), BF),
                pltpu.VMEM((cols, ROW, LANES), F32),
                pltpu.VMEM((cols, ROW, LANES), F32),
                pltpu.VMEM((size, group), F32),
                pltpu.VMEM((size, group), F32),
                pltpu.VMEM((size, group), F32),
                pltpu.VMEM((size, group), F32),
                pltpu.VMEM((3, size, group), BF),
                pltpu.VMEM((3, size, group), BF),
            ],
            input_output_aliases={len(fixed) + place: place for place in range(len(carried))},
        )(*fixed, *carried)
        arrived = exchange(partial, "context", outer)
        partials.append(jnp.sum(arrived.astype(F32), axis=0))

    total = jnp.stack(partials)
    med = total[:, :block].reshape(parts, n_dp, taps_own, group)
    extra = jnp.broadcast_to(total[:, None, block:], (parts, n_dp, held_short, group))
    sent = jnp.concatenate([med, extra], axis=2).reshape(parts * n_dp, taps_own + held_short, group)
    final = jnp.sum(exchange(sent, ("context", "dp"), both), axis=0)
    grad_med = final[:taps_own].T
    grad_short = final[taps_own : taps_own + 3 * width].reshape(3, width, group).transpose(0, 2, 1)
    return (*outs, grad_med, grad_short)


def solution(mesh):
    tokens = P("dp", "context", None)
    filters = (P("context", "dp"), P(None, "context", None))
    inner = functools.partial(per_device, mesh.shape["context"], mesh.shape["dp"])

    return jax.shard_map(
        inner,
        mesh=mesh,
        in_specs=(tokens,) * 4 + filters,
        out_specs=(tokens,) * 4 + filters,
        check_vma=False,
    )
```

```python
import functools

import jax
import jax.numpy as jnp
import numpy as np
from jax import lax
from jax.experimental import pallas as pl
from jax.experimental.pallas import tpu as pltpu
from jax.sharding import PartitionSpec as P


PARTS = 4
CHUNKS = ((0, 2), (2, 2))
BF = jnp.bfloat16
F32 = jnp.float32
LANES = 128
ROW = 8


def phases(tokens, size):
    angle = 2.0 * np.pi * (np.arange(size // 2)[:, None] + 0.5) * tokens[None, :] / size
    return np.concatenate([np.cos(angle), np.sin(angle)], axis=0)


def split_host(table):
    high = table.astype(BF)
    low = (table - high.astype(np.float64)).astype(BF)
    return jnp.asarray(high), jnp.asarray(low)


def transforms(block, width):
    size = 2 * block
    reach = width - 1
    own = np.arange(block)
    behind = np.where(own < reach, own + block, own - block)
    ahead = own + block
    rows = np.arange(block + ROW)
    forward = [
        split_host(phases(np.concatenate([own, behind]), size)),
        split_host(phases(own, size)),
        split_host(phases(ahead, size)),
    ]
    inverse = split_host(phases(rows, size).T * (2.0 / size))
    return forward, inverse


def split_bf(x):
    high = x.astype(BF)
    low = (x - high.astype(F32)).astype(BF)
    return high, low


def dot(a, b):
    return jnp.dot(a, b, preferred_element_type=F32)


def row_of(ref, index, col):
    per = ref.shape[2] // LANES
    return ref[col // per, pl.ds(index, 1), pl.ds(col % per * LANES, LANES)]


def load_padded(dst, own_ref, before, after, lanes, block):
    dst[pl.ds(0, ROW), :] = before
    dst[pl.ds(ROW, block), :] = own_ref[0, :, lanes].astype(F32)
    dst[pl.ds(ROW + block, ROW), :] = after


def causal(src, taps, first, width, col, rows):
    total = None
    for offset in range(width):
        term = row_of(taps, first + offset, col) * src[pl.ds(ROW - offset, rows), :]
        total = term if total is None else total + term
    return total


def make_products(block, width, cols, q, k, v, go, back, fore, taps, u_out, dz_out, x_q, x_k, x_v):
    for col in range(cols):
        lanes = pl.ds(col * LANES, LANES)
        for which, (src, dst) in enumerate(((q, x_q), (k, x_k), (v, x_v))):
            load_padded(
                dst.at[col],
                src,
                back[which, :, lanes].astype(F32),
                fore[which, :, lanes].astype(F32),
                lanes,
                block,
            )
        k_s = causal(x_k.at[col], taps, width, width, col, block)
        v_s = causal(x_v.at[col], taps, 2 * width, width, col, block)
        u_out[:, lanes] = (k_s * v_s).astype(BF)
        q_s = causal(x_q.at[col], taps, 0, width, col, block + ROW)
        dz_out[0:block, lanes] = (go[0, :, lanes].astype(F32) * q_s[0:block]).astype(BF)
        dz_out[block : block + ROW, lanes] = (
            fore[3, :, lanes].astype(F32) * q_s[block : block + ROW]
        ).astype(BF)


def mixer(
    block,
    width,
    cols,
    q,
    k,
    v,
    go,
    back,
    fore,
    taps,
    u_prev,
    dz_next,
    h_ref,
    fx_hi,
    fx_lo,
    fo_hi,
    fo_lo,
    fa_hi,
    fa_lo,
    in_hi,
    in_lo,
    *rest,
):
    rest = rest[len(rest) - 26 :]
    (
    mixed,
    g_q,
    g_k,
    g_v,
    g_part,
    sums,
    x_q,
    x_k,
    x_v,
    s_q,
    s_k,
    s_v,
    g_pad,
    h_pad,
    h_flip,
    z_pad,
    window,
    dz_own,
    edge_u,
    edge_z,
    spec_u,
    spec_h,
    spec_d,
    spec_w,
    prod_hi,
    prod_lo,
    ) = rest
    rows = block + ROW
    half = block
    rank = lax.broadcasted_iota(jnp.int32, (ROW, LANES), 0)
    for col in range(cols):
        lanes = pl.ds(col * LANES, LANES)
        for which, (src, dst) in enumerate(((q, x_q), (k, x_k), (v, x_v))):
            load_padded(
                dst.at[col],
                src,
                back[which, :, lanes].astype(F32),
                fore[which, :, lanes].astype(F32),
                lanes,
                block,
            )
        q_s = causal(x_q.at[col], taps, 0, width, col, rows)
        s_q[col] = q_s
        dz = (go[0, :, lanes].astype(F32) * q_s[0:block]).astype(BF)
        dz_own[:, lanes] = dz
        z_pad[col, 0:ROW, :] = jnp.zeros((ROW, LANES), F32)
        z_pad[col, ROW : 2 * ROW, :] = dz[0:ROW].astype(F32)
        k_s = causal(x_k.at[col], taps, width, width, col, rows)
        s_k[col] = k_s
        v_s = causal(x_v.at[col], taps, 2 * width, width, col, rows)
        s_v[col] = v_s
        u = (k_s * v_s).astype(BF)
        window[0:block, lanes] = u[0:block]
        u_after = u[block:rows].astype(F32)
        first = u_prev[0 : 2 * ROW, lanes]
        u_before = first.astype(F32)[0:ROW]
        patched = jnp.where(rank < width - 1, u_after, u_before)
        window[block : block + 2 * ROW, lanes] = jnp.concatenate(
            [patched, first.astype(F32)[ROW : 2 * ROW]], axis=0
        ).astype(BF)
        window[block + 2 * ROW : 2 * block, lanes] = u_prev[2 * ROW : block, lanes]
        edge_u[col] = u_before + u_after
        edge_z[col] = dz_next[block : block + ROW, lanes].astype(F32) + dz[0:ROW].astype(F32)
        taps_h = h_ref[0, :, lanes].astype(F32)
        h_pad[col, 0 : 2 * ROW, :] = taps_h[block - 2 * ROW : block]
        h_pad[col, 2 * ROW : 3 * ROW, :] = jnp.zeros((ROW, LANES), F32)
        h_flip[col, 0:ROW, :] = jnp.zeros((ROW, LANES), F32)
        for place in range(ROW):
            h_flip[col, ROW + place : ROW + place + 1, :] = h_pad[
                col, 2 * ROW - 1 - place : 2 * ROW - place, :
            ]

    x = window[...]
    spec_u[...] = dot(fx_hi[...], x) + dot(fx_lo[...], x)
    h = h_ref[0]
    spec_h[...] = dot(fo_hi[...], h) + dot(fo_lo[...], h)
    d = dz_own[...]
    spec_d[...] = dot(fo_hi[...], d) + dot(fo_lo[...], d)
    a = dz_next[0:block, :]
    spec_w[...] = spec_d[...] + (dot(fa_hi[...], a) + dot(fa_lo[...], a))

    def inverse(slot, count):
        high, low = prod_hi[slot], prod_lo[slot]
        top, rest = in_hi[0:count, :], in_lo[0:count, :]
        return dot(top, high) + (dot(rest, high) + dot(top, low))

    def store(slot, cos_part, sin_part):
        for place, part in ((0, cos_part), (half, sin_part)):
            high, low = split_bf(part)
            prod_hi[slot, place : place + half, :] = high
            prod_lo[slot, place : place + half, :] = low

    uc, us = spec_u[0:half, :], spec_u[half:, :]
    hc, hs = spec_h[0:half, :], spec_h[half:, :]
    store(0, uc * hc - us * hs, uc * hs + us * hc)
    wc, ws = spec_w[0:half, :], spec_w[half:, :]
    store(1, wc * hc + ws * hs, ws * hc - wc * hs)
    dc, ds = spec_d[0:half, :], spec_d[half:, :]
    store(2, dc * uc + ds * us, ds * uc - dc * us)

    z_all = inverse(0, rows)
    du_all = inverse(1, rows)
    gm_all = inverse(2, block)

    for col in range(cols):
        lanes = pl.ds(col * LANES, LANES)
        lo, hi = col * LANES, (col + 1) * LANES
        z = z_all[:, lo:hi]
        du = du_all[:, lo:hi]
        gm = gm_all[:, lo:hi]
        z_fix = jnp.zeros((ROW, LANES), F32)
        g_fix = jnp.zeros((ROW, LANES), F32)
        for place in range(1, width - 1):
            held = edge_u[col, place : place + 1, :]
            z_fix = z_fix + held * h_pad[col, pl.ds(2 * ROW - place, ROW), :]
            g_fix = g_fix + held * z_pad[col, pl.ds(place, ROW), :]
        du_fix = jnp.zeros((ROW, LANES), F32)
        for place in range(width - 2):
            held = edge_z[col, place : place + 1, :]
            du_fix = du_fix + held * h_flip[col, pl.ds(ROW - 1 - place, ROW), :]
        z = jnp.concatenate([z[0:ROW] + z_fix, z[ROW:]], axis=0)
        du = jnp.concatenate([du[0:block], du[block:] + du_fix], axis=0)
        gm = jnp.concatenate([gm[0 : block - ROW], gm[block - ROW : block] + g_fix], axis=0)
        g_part[0, 0, 0:block, lanes] = gm.astype(BF)
        mixed[0, :, lanes] = (s_q[col, 0:block, :] * z[0:block]).astype(BF)
        g_pad[0, 0:block, :] = go[0, :, lanes].astype(F32) * z[0:block]
        g_pad[0, block:rows, :] = fore[3, :, lanes].astype(F32) * z[block:rows]
        g_pad[1] = du * s_v[col]
        g_pad[2] = du * s_k[col]
        for which, (src, out) in enumerate(((x_q, g_q), (x_k, g_k), (x_v, g_v))):
            values = src[col, ROW : ROW + block, :]
            total = None
            for offset in range(width):
                moved = g_pad[which, pl.ds(offset, block), :]
                term = row_of(taps, which * width + offset, col) * moved
                total = term if total is None else total + term
                place = which * width + offset
                sums[place : place + 1, :] = jnp.sum(values * moved, axis=0, keepdims=True)
            out[0, :, lanes] = total.astype(BF)
        g_part[0, 0, block : block + 3 * ROW, lanes] = sums[...].astype(BF)


def halo_pairs(count):
    return [(i, i + 1) for i in range(count - 1)], [(i + 1, i) for i in range(count - 1)]


def groups_of(n_context, n_dp, fine):
    coarse = n_context // fine
    inner = [[c * fine + f for f in range(fine)] for c in range(coarse)]
    outer = [[c * fine + f for c in range(coarse)] for f in range(fine)]
    both = [
        [(c * fine + f) * n_dp + d for f in range(fine) for d in range(n_dp)] for c in range(coarse)
    ]
    return inner, outer, both


def exchange(x, axes, groups=None):
    return lax.all_to_all(x, axes, 0, 0, axis_index_groups=groups)


def spread(x, count, axes, groups=None):
    return exchange(jnp.broadcast_to(x, (count,) + x.shape), axes, groups)


def per_device(n_context, n_dp, query_in, key_in, value_in, grad_out, med_filter, short_filter):
    _, block, _ = query_in.shape
    group, taps_own = med_filter.shape
    width = short_filter.shape[2]
    size = 2 * block
    rows = block + ROW
    held_short = 3 * ROW
    parts = PARTS
    coarse = n_context // parts
    ahead, behind = halo_pairs(n_context)
    _, outer, both = groups_of(n_context, n_dp, parts)
    forward, inverse = transforms(block, width)
    tables = [part for pair in forward + [inverse] for part in pair]

    mine = spread(med_filter.astype(BF).T, parts * n_dp, ("context", "dp"), both)
    mine = mine.reshape(parts, block, group)

    back = jnp.concatenate([x[:, block - ROW :] for x in (query_in, key_in, value_in)], axis=0)
    fore = jnp.concatenate([x[:, :ROW] for x in (query_in, key_in, value_in, grad_out)], axis=0)
    back = lax.ppermute(back, "context", ahead)
    fore = lax.ppermute(fore, "context", behind)

    short = short_filter.transpose(0, 2, 1).reshape(3 * width, group)
    short = jnp.pad(short, ((0, held_short - 3 * width), (0, 0)))
    taps = spread(short, n_context, "context")
    h_all = spread(mine, coarse, "context", outer)

    whole = lambda x: pl.BlockSpec(x.shape, lambda *_: (0,) * x.ndim)
    pieces = []
    for first, count in CHUNKS:
        wide = count * group
        per = parts // count
        place = first // count
        cols = wide // LANES
        padded = pltpu.VMEM((cols, block + 2 * ROW, LANES), F32)
        at = lambda i, per=per, place=place: per * i + place
        tokens = pl.BlockSpec((1, block, wide), lambda i, at=at: (0, 0, at(i)))
        stack = lambda height, at=at: pl.BlockSpec((height, ROW, wide), lambda i: (0, 0, at(i)))
        filters = pl.BlockSpec((count, held_short, group), lambda i, at=at: (at(i), 0, 0))
        packed = lambda height: pl.BlockSpec((height, wide), lambda i: (0, i))
        u, dz = pl.pallas_call(
            functools.partial(make_products, block, width, cols),
            grid=(coarse,),
            in_specs=[tokens] * 4 + [stack(3), stack(4), filters],
            out_specs=[packed(block), packed(rows)],
            out_shape=[
                jax.ShapeDtypeStruct((block, coarse * wide), BF),
                jax.ShapeDtypeStruct((rows, coarse * wide), BF),
            ],
            scratch_shapes=[padded] * 3,
        )(query_in, key_in, value_in, grad_out, back, fore, taps)
        u_prev = lax.ppermute(u, "context", ahead)
        dz_next = lax.ppermute(dz, "context", behind)
        pieces.append((u_prev, dz_next))

    outs = None
    partials = []
    cols = group // LANES
    padded = pltpu.VMEM((cols, block + 2 * ROW, LANES), F32)
    shifted = pltpu.VMEM((cols, rows, LANES), F32)
    for index, (first, count) in enumerate(CHUNKS):
        at = lambda i, j, first=first: parts * i + first + j
        tokens = pl.BlockSpec((1, block, group), lambda i, j, at=at: (0, 0, at(i, j)))
        stack = lambda height, at=at: pl.BlockSpec(
            (height, ROW, group), lambda i, j: (0, 0, at(i, j))
        )
        filters = pl.BlockSpec((1, held_short, group), lambda i, j, at=at: (at(i, j), 0, 0))
        packed = lambda height, count=count: pl.BlockSpec(
            (height, group), lambda i, j: (0, count * i + j)
        )
        taps_h = pl.BlockSpec(
            (1, None, block, group), lambda i, j, first=first: (i, first + j, 0, 0)
        )
        u_prev, dz_next = pieces[index]
        carried = [] if outs is None else list(outs)
        fixed = [query_in, key_in, value_in, grad_out, back, fore, taps, u_prev, dz_next]
        fixed += [h_all, *tables]
        *outs, partial = pl.pallas_call(
            functools.partial(mixer, block, width, cols),
            grid=(coarse, count),
            in_specs=[tokens] * 4
            + [stack(3), stack(4), filters, packed(block), packed(rows), taps_h]
            + [whole(x) for x in tables]
            + [pl.BlockSpec(memory_space=pl.ANY)] * len(carried),
            out_specs=[tokens] * 4
            + [pl.BlockSpec((1, 1, block + held_short, group), lambda i, j: (i, j, 0, 0))],
            out_shape=[jax.ShapeDtypeStruct(query_in.shape, BF)] * 4
            + [jax.ShapeDtypeStruct((coarse, count, block + held_short, group), BF)],
            scratch_shapes=[
                pltpu.VMEM((held_short, LANES), F32),
                padded,
                padded,
                padded,
                shifted,
                shifted,
                shifted,
                pltpu.VMEM((3, rows, LANES), F32),
                pltpu.VMEM((cols, 3 * ROW, LANES), F32),
                pltpu.VMEM((cols, 2 * ROW, LANES), F32),
                pltpu.VMEM((cols, 2 * ROW, LANES), F32),
                pltpu.VMEM((size, group), BF),
                pltpu.VMEM((block, group), BF),
                pltpu.VMEM((cols, ROW, LANES), F32),
                pltpu.VMEM((cols, ROW, LANES), F32),
                pltpu.VMEM((size, group), F32),
                pltpu.VMEM((size, group), F32),
                pltpu.VMEM((size, group), F32),
                pltpu.VMEM((size, group), F32),
                pltpu.VMEM((3, size, group), BF),
                pltpu.VMEM((3, size, group), BF),
            ],
            input_output_aliases={len(fixed) + k: k for k in range(len(carried))},
        )(*fixed, *carried)
        arrived = exchange(partial, "context", outer)
        partials.append(jnp.sum(arrived.astype(F32), axis=0))

    total = jnp.concatenate(partials, axis=0).astype(BF)
    med = total[:, :block].reshape(parts, n_dp, taps_own, group)
    extra = jnp.broadcast_to(total[:, None, block:], (parts, n_dp, held_short, group))
    sent = jnp.concatenate([med, extra], axis=2).reshape(parts * n_dp, taps_own + held_short, group)
    sent = exchange(sent, ("context", "dp"), both)
    final = jnp.sum(sent.astype(F32), axis=0)
    grad_med = final[:taps_own].T
    grad_short = final[taps_own : taps_own + 3 * width].reshape(3, width, group).transpose(0, 2, 1)
    return (*outs, grad_med, grad_short)


def solution(mesh):
    tokens = P("dp", "context", None)
    filters = (P("context", "dp"), P(None, "context", None))
    inner = functools.partial(per_device, mesh.shape["context"], mesh.shape["dp"])

    return jax.shard_map(
        inner,
        mesh=mesh,
        in_specs=(tokens,) * 4 + filters,
        out_specs=(tokens,) * 4 + filters,
        check_vma=False,
    )
```

```python
import functools

import jax
import jax.numpy as jnp
import numpy as np
from jax import lax
from jax.experimental import pallas as pl
from jax.experimental.pallas import tpu as pltpu
from jax.sharding import PartitionSpec as P


PARTS = 4
CHUNKS = ((0, 2), (2, 2))
BF = jnp.bfloat16
F32 = jnp.float32
LANES = 128
ROW = 8
TALL = 64


def phases(tokens, size):
    angle = 2.0 * np.pi * (np.arange(size // 2)[:, None] + 0.5) * tokens[None, :] / size
    return np.concatenate([np.cos(angle), np.sin(angle)], axis=0)


def split_host(table):
    high = table.astype(BF)
    low = (table - high.astype(np.float64)).astype(BF)
    return jnp.asarray(np.concatenate([high, low], axis=1))


def transforms(block, width):
    size = 2 * block
    reach = width - 1
    own = np.arange(block)
    behind = np.where(own < reach, own + block, own - block)
    ahead = own + block
    rows = np.arange(block + ROW)
    forward = [
        split_host(phases(np.concatenate([own, behind]), size)),
        split_host(phases(own, size)),
        split_host(phases(ahead, size)),
    ]
    inverse = split_host(phases(rows, size).T * (2.0 / size))
    return forward, inverse


def dot(a, b):
    return jnp.dot(a, b, preferred_element_type=F32)


def dot_twice(high_low, b):
    return dot(high_low, jnp.concatenate([b, b], axis=0))


def row_of(ref, index, col):
    per = ref.shape[2] // LANES
    return ref[col // per, pl.ds(index, 1), pl.ds(col % per * LANES, LANES)]


def load_padded(dst, own_ref, before, after, lanes, block):
    dst[pl.ds(0, ROW), :] = before
    dst[pl.ds(ROW, block), :] = own_ref[0, :, lanes].astype(F32)
    dst[pl.ds(ROW + block, ROW), :] = after


def causal(src, taps, first, width, col, rows):
    total = None
    for offset in range(width):
        term = row_of(taps, first + offset, col) * src[pl.ds(ROW - offset, rows), :]
        total = term if total is None else total + term
    return total


def make_products(block, width, cols, q, k, v, go, back, fore, taps, u_out, dz_out, x_q, x_k, x_v):
    for col in range(cols):
        lanes = pl.ds(col * LANES, LANES)
        for which, (src, dst) in enumerate(((q, x_q), (k, x_k), (v, x_v))):
            load_padded(
                dst.at[col],
                src,
                back[which, :, lanes].astype(F32),
                fore[which, :, lanes].astype(F32),
                lanes,
                block,
            )
        k_s = causal(x_k.at[col], taps, width, width, col, block)
        v_s = causal(x_v.at[col], taps, 2 * width, width, col, block)
        u_out[:, lanes] = (k_s * v_s).astype(BF)
        q_s = causal(x_q.at[col], taps, 0, width, col, block + ROW)
        dz_out[0:block, lanes] = (go[0, :, lanes].astype(F32) * q_s[0:block]).astype(BF)
        dz_out[block : block + ROW, lanes] = (
            fore[3, :, lanes].astype(F32) * q_s[block : block + ROW]
        ).astype(BF)


def mixer(block, width, subs, q, k, v, go, back, fore, taps, u_prev, dz_next, h_ref, *rest):
    rows = block + ROW
    half = block
    per = q.shape[2] // LANES // subs
    group = per * LANES
    t_window, t_own, t_ahead, t_inverse = rest[:4]
    outs = rest[len(rest) - 24 :]
    mixed, g_q, g_k, g_v, g_part, sums, x_q, x_k, x_v, s_q, s_k, s_v, g_pad = outs[:13]
    h_pad, h_flip, z_pad, window, dz_own, edge_u, edge_z, spec_u, spec_h, spec_d, spec_w = outs[13:]
    rank = lax.broadcasted_iota(jnp.int32, (ROW, LANES), 0)

    def gather_rows(sub, col):
        lanes = pl.ds(col * LANES, LANES)
        inside = pl.ds((col - sub * per) * LANES, LANES)
        for which, (src, dst) in enumerate(((q, x_q), (k, x_k), (v, x_v))):
            load_padded(
                dst.at[col],
                src,
                back[which, :, lanes].astype(F32),
                fore[which, :, lanes].astype(F32),
                lanes,
                block,
            )
        q_s = causal(x_q.at[col], taps, 0, width, col, rows)
        s_q[col] = q_s
        dz = (go[0, :, lanes].astype(F32) * q_s[0:block]).astype(BF)
        dz_own[sub, :, inside] = dz
        z_pad[col, 0:ROW, :] = jnp.zeros((ROW, LANES), F32)
        z_pad[col, ROW : 2 * ROW, :] = dz[0:ROW].astype(F32)
        k_s = causal(x_k.at[col], taps, width, width, col, rows)
        s_k[col] = k_s
        v_s = causal(x_v.at[col], taps, 2 * width, width, col, rows)
        s_v[col] = v_s
        u = (k_s * v_s).astype(BF)
        window[sub, 0:block, inside] = u[0:block]
        u_after = u[block:rows].astype(F32)
        first = u_prev[0 : 2 * ROW, lanes].astype(F32)
        u_before = first[0:ROW]
        patched = jnp.where(rank < width - 1, u_after, u_before)
        window[sub, block : block + 2 * ROW, inside] = jnp.concatenate(
            [patched, first[ROW : 2 * ROW]], axis=0
        ).astype(BF)
        window[sub, block + 2 * ROW : 2 * block, inside] = u_prev[2 * ROW : block, lanes]
        edge_u[col] = u_before + u_after
        edge_z[col] = dz_next[block : block + ROW, lanes].astype(F32) + dz[0:ROW].astype(F32)
        h_pad[col, 0 : 2 * ROW, :] = h_ref[0, sub, block - 2 * ROW : block, inside].astype(F32)
        h_pad[col, 2 * ROW : 3 * ROW, :] = jnp.zeros((ROW, LANES), F32)
        h_flip[col, 0:ROW, :] = jnp.zeros((ROW, LANES), F32)
        for place in range(width - 2):
            h_flip[col, ROW + place : ROW + place + 1, :] = h_pad[
                col, 2 * ROW - 1 - place : 2 * ROW - place, :
            ]

    def spectra(sub):
        lanes = pl.ds(sub * group, group)
        x = window[sub]
        spec_u[sub] = dot_twice(t_window[...], x)
        h = h_ref[0, sub]
        spec_h[sub] = dot_twice(t_own[...], h)
        d = dz_own[sub]
        spec_d[sub] = dot_twice(t_own[...], d)
        a = dz_next[0:block, lanes]
        spec_w[sub] = spec_d[sub] + dot_twice(t_ahead[...], a)

    def inverse(cos_part, sin_part, count):
        high = jnp.concatenate([cos_part.astype(BF), sin_part.astype(BF)], axis=0)
        return dot_twice(t_inverse[0:count, :], high)

    def times(sub, lanes):
        uc, us = spec_u[sub, 0:half, lanes], spec_u[sub, half:, lanes]
        hc, hs = spec_h[sub, 0:half, lanes], spec_h[sub, half:, lanes]
        z = inverse(uc * hc - us * hs, uc * hs + us * hc, rows)
        wc, ws = spec_w[sub, 0:half, lanes], spec_w[sub, half:, lanes]
        du = inverse(wc * hc + ws * hs, ws * hc - wc * hs, rows)
        dc, ds = spec_d[sub, 0:half, lanes], spec_d[sub, half:, lanes]
        gm = inverse(dc * uc + ds * us, ds * uc - dc * us, block)
        return z, du, gm

    def finish(sub, col, z, du, gm):
        lanes = pl.ds(col * LANES, LANES)
        inside = pl.ds((col - sub * per) * LANES, LANES)
        z_fix = jnp.zeros((ROW, LANES), F32)
        g_fix = jnp.zeros((ROW, LANES), F32)
        for place in range(1, width - 1):
            held = edge_u[col, place : place + 1, :]
            z_fix = z_fix + held * h_pad[col, pl.ds(2 * ROW - place, ROW), :]
            g_fix = g_fix + held * z_pad[col, pl.ds(place, ROW), :]
        du_fix = jnp.zeros((ROW, LANES), F32)
        for place in range(width - 2):
            held = edge_z[col, place : place + 1, :]
            du_fix = du_fix + held * h_flip[col, pl.ds(ROW - 1 - place, ROW), :]
        z = jnp.concatenate([z[0:ROW] + z_fix, z[ROW:]], axis=0)
        du = jnp.concatenate([du[0:block], du[block:] + du_fix], axis=0)
        gm = jnp.concatenate([gm[0 : block - ROW], gm[block - ROW : block] + g_fix], axis=0)
        g_part[0, sub, 0:block, inside] = gm.astype(BF)
        mixed[0, :, lanes] = (s_q[col, 0:block, :] * z[0:block]).astype(BF)
        g_pad[col, 0, 0:block, :] = go[0, :, lanes].astype(F32) * z[0:block]
        g_pad[col, 0, block:rows, :] = fore[3, :, lanes].astype(F32) * z[block:rows]
        g_pad[col, 1] = du * s_v[col]
        g_pad[col, 2] = du * s_k[col]
        for which, (src, out) in enumerate(((x_q, g_q), (x_k, g_k), (x_v, g_v))):
            for start in range(0, block, TALL):
                values = src[col, ROW + start : ROW + start + TALL, :]
                total = None
                for offset in range(width):
                    moved = g_pad[col, which, pl.ds(start + offset, TALL), :]
                    term = row_of(taps, which * width + offset, col) * moved
                    total = term if total is None else total + term
                    weight = values * moved
                    held = weight[0:ROW]
                    for r in range(ROW, TALL, ROW):
                        held = held + weight[r : r + ROW]
                    place = which * width + offset
                    if start == 0:
                        sums[col, place] = held
                    else:
                        sums[col, place] = sums[col, place] + held
                out[0, start : start + TALL, lanes] = total.astype(BF)
        g_part[0, sub, block : block + 3 * ROW, inside] = jnp.sum(sums[col], axis=1).astype(BF)

    for sub in range(subs):
        for col in range(sub * per, (sub + 1) * per):
            gather_rows(sub, col)
        spectra(sub)
    for sub in range(subs):
        found = times(sub, pl.ds(0, group))
        for col in range(sub * per, (sub + 1) * per):
            lo = (col - sub * per) * LANES
            finish(sub, col, *(x[:, lo : lo + LANES] for x in found))


def halo_pairs(count):
    return [(i, i + 1) for i in range(count - 1)], [(i + 1, i) for i in range(count - 1)]


def groups_of(n_context, n_dp, fine):
    coarse = n_context // fine
    inner = [[c * fine + f for f in range(fine)] for c in range(coarse)]
    outer = [[c * fine + f for c in range(coarse)] for f in range(fine)]
    both = [
        [(c * fine + f) * n_dp + d for f in range(fine) for d in range(n_dp)] for c in range(coarse)
    ]
    return inner, outer, both


def exchange(x, axes, groups=None):
    return lax.all_to_all(x, axes, 0, 0, axis_index_groups=groups)


def spread(x, count, axes, groups=None):
    return exchange(jnp.broadcast_to(x, (count,) + x.shape), axes, groups)


def per_device(n_context, n_dp, query_in, key_in, value_in, grad_out, med_filter, short_filter):
    _, block, _ = query_in.shape
    group, taps_own = med_filter.shape
    width = short_filter.shape[2]
    size = 2 * block
    rows = block + ROW
    held_short = 3 * ROW
    parts = PARTS
    coarse = n_context // parts
    ahead, behind = halo_pairs(n_context)
    inner, outer, both = groups_of(n_context, n_dp, parts)
    forward, inverse = transforms(block, width)
    tables = forward + [inverse]

    back = jnp.concatenate([x[:, block - ROW :] for x in (query_in, key_in, value_in)], axis=0)
    fore = jnp.concatenate([x[:, :ROW] for x in (query_in, key_in, value_in, grad_out)], axis=0)
    back = lax.ppermute(back, "context", ahead)
    fore = lax.ppermute(fore, "context", behind)

    short = short_filter.transpose(0, 2, 1).reshape(3 * width, group)
    short = jnp.pad(short, ((0, held_short - 3 * width), (0, 0)))
    taps = spread(short, n_context, "context")
    mine = lax.all_gather(med_filter.astype(BF).T, "dp", axis=0, tiled=True)
    mine = spread(mine, parts, "context", inner)
    h_all = spread(mine, coarse, "context", outer)

    whole = lambda x: pl.BlockSpec(x.shape, lambda *_: (0,) * x.ndim)
    pieces = []
    for first, count in CHUNKS:
        wide = count * group
        per = parts // count
        place = first // count
        cols = wide // LANES
        padded = pltpu.VMEM((cols, block + 2 * ROW, LANES), F32)
        at = lambda i, per=per, place=place: per * i + place
        tokens = pl.BlockSpec((1, block, wide), lambda i, at=at: (0, 0, at(i)))
        stack = lambda height, at=at: pl.BlockSpec((height, ROW, wide), lambda i: (0, 0, at(i)))
        filters = pl.BlockSpec((count, held_short, group), lambda i, at=at: (at(i), 0, 0))
        packed = lambda height: pl.BlockSpec((height, wide), lambda i: (0, i))
        u, dz = pl.pallas_call(
            functools.partial(make_products, block, width, cols),
            grid=(coarse,),
            in_specs=[tokens] * 4 + [stack(3), stack(4), filters],
            out_specs=[packed(block), packed(rows)],
            out_shape=[
                jax.ShapeDtypeStruct((block, coarse * wide), BF),
                jax.ShapeDtypeStruct((rows, coarse * wide), BF),
            ],
            scratch_shapes=[padded] * 3,
        )(query_in, key_in, value_in, grad_out, back, fore, taps)
        u_prev = lax.ppermute(u, "context", ahead)
        dz_next = lax.ppermute(dz, "context", behind)
        pieces.append((u_prev, dz_next))

    outs = None
    partials = []
    for index, (first, count) in enumerate(CHUNKS):
        wide = count * group
        per = parts // count
        place = first // count
        cols = wide // LANES
        at = lambda i, per=per, place=place: per * i + place
        tokens = pl.BlockSpec((1, block, wide), lambda i, at=at: (0, 0, at(i)))
        stack = lambda height, at=at: pl.BlockSpec((height, ROW, wide), lambda i: (0, 0, at(i)))
        filters = pl.BlockSpec((count, held_short, group), lambda i, at=at: (at(i), 0, 0))
        packed = lambda height: pl.BlockSpec((height, wide), lambda i: (0, i))
        taps_h = pl.BlockSpec((1, count, block, group), lambda i, place=place: (i, place, 0, 0))
        padded = pltpu.VMEM((cols, block + 2 * ROW, LANES), F32)
        shifted = pltpu.VMEM((cols, rows, LANES), F32)
        strip = lambda height: pltpu.VMEM((cols, height * ROW, LANES), F32)
        spectrum = pltpu.VMEM((count, size, group), F32)
        u_prev, dz_next = pieces[index]
        carried = [] if outs is None else list(outs)
        fixed = [query_in, key_in, value_in, grad_out, back, fore, taps, u_prev, dz_next]
        fixed += [h_all, *tables]
        *outs, partial = pl.pallas_call(
            functools.partial(mixer, block, width, count),
            grid=(coarse,),
            in_specs=[tokens] * 4
            + [stack(3), stack(4), filters, packed(block), packed(rows), taps_h]
            + [whole(x) for x in tables]
            + [pl.BlockSpec(memory_space=pl.ANY)] * len(carried),
            out_specs=[tokens] * 4
            + [pl.BlockSpec((1, count, block + held_short, group), lambda i: (i, 0, 0, 0))],
            out_shape=[jax.ShapeDtypeStruct(query_in.shape, BF)] * 4
            + [jax.ShapeDtypeStruct((coarse, count, block + held_short, group), BF)],
            scratch_shapes=[
                pltpu.VMEM((cols, held_short, ROW, LANES), F32),
                padded,
                padded,
                padded,
                shifted,
                shifted,
                shifted,
                pltpu.VMEM((cols, 3, rows, LANES), F32),
                strip(3),
                strip(2),
                strip(2),
                pltpu.VMEM((count, size, group), BF),
                pltpu.VMEM((count, block, group), BF),
                strip(1),
                strip(1),
                spectrum,
                spectrum,
                spectrum,
                spectrum,
            ],
            input_output_aliases={len(fixed) + k: k for k in range(len(carried))},
        )(*fixed, *carried)
        arrived = exchange(partial, "context", outer)
        partials.append(jnp.sum(arrived.astype(F32), axis=0))

    total = jnp.concatenate(partials, axis=0).astype(BF)
    med = total[:, :block].reshape(parts, n_dp, taps_own, group)
    extra = jnp.broadcast_to(total[:, None, block:], (parts, n_dp, held_short, group))
    sent = jnp.concatenate([med, extra], axis=2).reshape(parts * n_dp, taps_own + held_short, group)
    sent = exchange(sent, ("context", "dp"), both)
    final = jnp.sum(sent.astype(F32), axis=0)
    grad_med = final[:taps_own].T
    grad_short = final[taps_own : taps_own + 3 * width].reshape(3, width, group).transpose(0, 2, 1)
    return (*outs, grad_med, grad_short)


def solution(mesh):
    tokens = P("dp", "context", None)
    filters = (P("context", "dp"), P(None, "context", None))
    inner = functools.partial(per_device, mesh.shape["context"], mesh.shape["dp"])

    return jax.shard_map(
        inner,
        mesh=mesh,
        in_specs=(tokens,) * 4 + filters,
        out_specs=(tokens,) * 4 + filters,
        check_vma=False,
    )
```

```python
import functools

import jax
import jax.numpy as jnp
import numpy as np
from jax import lax
from jax.experimental import pallas as pl
from jax.experimental.pallas import tpu as pltpu
from jax.sharding import PartitionSpec as P


PARTS = 4
CHUNKS = ((0, 2), (2, 2))
BF = jnp.bfloat16
F32 = jnp.float32
LANES = 128
ROW = 8
TALL = 64


def phases(tokens, size):
    angle = 2.0 * np.pi * (np.arange(size // 2)[:, None] + 0.5) * tokens[None, :] / size
    return np.concatenate([np.cos(angle), np.sin(angle)], axis=0)


def split_host(table):
    high = table.astype(BF)
    low = (table - high.astype(np.float64)).astype(BF)
    return jnp.asarray(np.concatenate([high, low], axis=1))


def transforms(block, width):
    size = 2 * block
    reach = width - 1
    own = np.arange(block)
    behind = np.where(own < reach, own + block, own - block)
    ahead = own + block
    rows = np.arange(block + ROW)
    forward = [
        split_host(phases(np.concatenate([own, behind]), size)),
        split_host(phases(own, size)),
        split_host(phases(ahead, size)),
    ]
    inverse = split_host(phases(rows, size).T * (2.0 / size))
    return forward, inverse


def dot(a, b):
    return jnp.dot(a, b, preferred_element_type=F32)


def dot_twice(high_low, b):
    return dot(high_low, jnp.concatenate([b, b], axis=0))


def row_of(ref, index, col):
    per = ref.shape[2] // LANES
    return ref[col // per, pl.ds(index, 1), pl.ds(col % per * LANES, LANES)]


def load_padded(dst, own_ref, before, after, lanes, block):
    dst[pl.ds(0, ROW), :] = before
    dst[pl.ds(ROW, block), :] = own_ref[0, :, lanes].astype(F32)
    dst[pl.ds(ROW + block, ROW), :] = after


def causal(src, taps, first, width, col, rows):
    total = None
    for offset in range(width):
        term = row_of(taps, first + offset, col) * src[pl.ds(ROW - offset, rows), :]
        total = term if total is None else total + term
    return total


def make_products(block, width, cols, q, k, v, go, back, fore, taps, u_out, dz_out, x_q, x_k, x_v):
    for col in range(cols):
        lanes = pl.ds(col * LANES, LANES)
        for which, (src, dst) in enumerate(((q, x_q), (k, x_k), (v, x_v))):
            load_padded(
                dst.at[col],
                src,
                back[which, :, lanes].astype(F32),
                fore[which, :, lanes].astype(F32),
                lanes,
                block,
            )
        k_s = causal(x_k.at[col], taps, width, width, col, block)
        v_s = causal(x_v.at[col], taps, 2 * width, width, col, block)
        u_out[:, lanes] = (k_s * v_s).astype(BF)
        q_s = causal(x_q.at[col], taps, 0, width, col, block + ROW)
        dz_out[0:block, lanes] = (go[0, :, lanes].astype(F32) * q_s[0:block]).astype(BF)
        dz_out[block : block + ROW, lanes] = (
            fore[3, :, lanes].astype(F32) * q_s[block : block + ROW]
        ).astype(BF)


def mixer(block, width, subs, q, k, v, go, back, fore, taps, u_prev, dz_next, h_ref, *rest):
    rows = block + ROW
    half = block
    per = q.shape[2] // LANES // subs
    group = per * LANES
    t_window, t_own, t_ahead, t_inverse = rest[:4]
    outs = rest[len(rest) - 24 :]
    mixed, g_q, g_k, g_v, g_part, sums, x_q, x_k, x_v, s_q, s_k, s_v, g_pad = outs[:13]
    h_pad, h_flip, z_pad, window, dz_own, edge_u, edge_z, spec_u, spec_h, spec_d, spec_w = outs[13:]
    rank = lax.broadcasted_iota(jnp.int32, (ROW, LANES), 0)

    def gather_rows(sub, col):
        lanes = pl.ds(col * LANES, LANES)
        inside = pl.ds((col - sub * per) * LANES, LANES)
        for which, (src, dst) in enumerate(((q, x_q), (k, x_k), (v, x_v))):
            load_padded(
                dst.at[col],
                src,
                back[which, :, lanes].astype(F32),
                fore[which, :, lanes].astype(F32),
                lanes,
                block,
            )
        q_s = causal(x_q.at[col], taps, 0, width, col, rows)
        s_q[col] = q_s
        dz = (go[0, :, lanes].astype(F32) * q_s[0:block]).astype(BF)
        dz_own[sub, :, inside] = dz
        z_pad[col, 0:ROW, :] = jnp.zeros((ROW, LANES), F32)
        z_pad[col, ROW : 2 * ROW, :] = dz[0:ROW].astype(F32)
        k_s = causal(x_k.at[col], taps, width, width, col, rows)
        s_k[col] = k_s
        v_s = causal(x_v.at[col], taps, 2 * width, width, col, rows)
        s_v[col] = v_s
        u = (k_s * v_s).astype(BF)
        window[sub, 0:block, inside] = u[0:block]
        u_after = u[block:rows].astype(F32)
        first = u_prev[0 : 2 * ROW, lanes].astype(F32)
        u_before = first[0:ROW]
        patched = jnp.where(rank < width - 1, u_after, u_before)
        window[sub, block : block + 2 * ROW, inside] = jnp.concatenate(
            [patched, first[ROW : 2 * ROW]], axis=0
        ).astype(BF)
        window[sub, block + 2 * ROW : 2 * block, inside] = u_prev[2 * ROW : block, lanes]
        edge_u[col] = u_before + u_after
        edge_z[col] = dz_next[block : block + ROW, lanes].astype(F32) + dz[0:ROW].astype(F32)
        h_pad[col, 0 : 2 * ROW, :] = h_ref[0, sub, block - 2 * ROW : block, inside].astype(F32)
        h_pad[col, 2 * ROW : 3 * ROW, :] = jnp.zeros((ROW, LANES), F32)
        h_flip[col, 0:ROW, :] = jnp.zeros((ROW, LANES), F32)
        for place in range(width - 2):
            h_flip[col, ROW + place : ROW + place + 1, :] = h_pad[
                col, 2 * ROW - 1 - place : 2 * ROW - place, :
            ]

    def spectra(sub):
        lanes = pl.ds(sub * group, group)
        x = window[sub]
        spec_u[sub] = dot_twice(t_window[...], x)
        h = h_ref[0, sub]
        spec_h[sub] = dot_twice(t_own[...], h)
        d = dz_own[sub]
        spec_d[sub] = dot_twice(t_own[...], d)
        a = dz_next[0:block, lanes]
        spec_w[sub] = spec_d[sub] + dot_twice(t_ahead[...], a)

    def inverse(cos_part, sin_part, count):
        high = jnp.concatenate([cos_part.astype(BF), sin_part.astype(BF)], axis=0)
        return dot_twice(t_inverse[0:count, :], high)

    def times(sub, lanes):
        uc, us = spec_u[sub, 0:half, lanes], spec_u[sub, half:, lanes]
        hc, hs = spec_h[sub, 0:half, lanes], spec_h[sub, half:, lanes]
        z = inverse(uc * hc - us * hs, uc * hs + us * hc, rows)
        wc, ws = spec_w[sub, 0:half, lanes], spec_w[sub, half:, lanes]
        du = inverse(wc * hc + ws * hs, ws * hc - wc * hs, rows)
        dc, ds = spec_d[sub, 0:half, lanes], spec_d[sub, half:, lanes]
        gm = inverse(dc * uc + ds * us, ds * uc - dc * us, block)
        return z, du, gm

    def finish(sub, col, z, du, gm):
        lanes = pl.ds(col * LANES, LANES)
        inside = pl.ds((col - sub * per) * LANES, LANES)
        z_fix = jnp.zeros((ROW, LANES), F32)
        g_fix = jnp.zeros((ROW, LANES), F32)
        for place in range(1, width - 1):
            held = edge_u[col, place : place + 1, :]
            z_fix = z_fix + held * h_pad[col, pl.ds(2 * ROW - place, ROW), :]
            g_fix = g_fix + held * z_pad[col, pl.ds(place, ROW), :]
        du_fix = jnp.zeros((ROW, LANES), F32)
        for place in range(width - 2):
            held = edge_z[col, place : place + 1, :]
            du_fix = du_fix + held * h_flip[col, pl.ds(ROW - 1 - place, ROW), :]
        z = jnp.concatenate([z[0:ROW] + z_fix, z[ROW:]], axis=0)
        du = jnp.concatenate([du[0:block], du[block:] + du_fix], axis=0)
        gm = jnp.concatenate([gm[0 : block - ROW], gm[block - ROW : block] + g_fix], axis=0)
        g_part[0, sub, 0:block, inside] = gm.astype(BF)
        mixed[0, :, lanes] = (s_q[col, 0:block, :] * z[0:block]).astype(BF)
        g_pad[col, 0, 0:block, :] = go[0, :, lanes].astype(F32) * z[0:block]
        g_pad[col, 0, block:rows, :] = fore[3, :, lanes].astype(F32) * z[block:rows]
        g_pad[col, 1] = du * s_v[col]
        g_pad[col, 2] = du * s_k[col]
        for which, (src, out) in enumerate(((x_q, g_q), (x_k, g_k), (x_v, g_v))):
            for start in range(0, block, TALL):
                values = src[col, ROW + start : ROW + start + TALL, :]
                total = None
                for offset in range(width):
                    moved = g_pad[col, which, pl.ds(start + offset, TALL), :]
                    term = row_of(taps, which * width + offset, col) * moved
                    total = term if total is None else total + term
                    weight = values * moved
                    held = weight[0:ROW]
                    for r in range(ROW, TALL, ROW):
                        held = held + weight[r : r + ROW]
                    place = which * width + offset
                    if start == 0:
                        sums[col, place] = held
                    else:
                        sums[col, place] = sums[col, place] + held
                out[0, start : start + TALL, lanes] = total.astype(BF)
        g_part[0, sub, block : block + 3 * ROW, inside] = jnp.sum(sums[col], axis=1).astype(BF)

    for sub in range(subs):
        for col in range(sub * per, (sub + 1) * per):
            gather_rows(sub, col)
        spectra(sub)
    for sub in range(subs):
        found = times(sub, pl.ds(0, group))
        for col in range(sub * per, (sub + 1) * per):
            lo = (col - sub * per) * LANES
            finish(sub, col, *(x[:, lo : lo + LANES] for x in found))


def halo_pairs(count):
    return [(i, i + 1) for i in range(count - 1)], [(i + 1, i) for i in range(count - 1)]


def groups_of(n_context, n_dp, fine):
    coarse = n_context // fine
    inner = [[c * fine + f for f in range(fine)] for c in range(coarse)]
    outer = [[c * fine + f for c in range(coarse)] for f in range(fine)]
    both = [
        [(c * fine + f) * n_dp + d for f in range(fine) for d in range(n_dp)] for c in range(coarse)
    ]
    return inner, outer, both


def exchange(x, axes, groups=None):
    return lax.all_to_all(x, axes, 0, 0, axis_index_groups=groups)


def spread(x, count, axes, groups=None):
    return exchange(jnp.broadcast_to(x, (count,) + x.shape), axes, groups)


def per_device(n_context, n_dp, query_in, key_in, value_in, grad_out, med_filter, short_filter):
    _, block, _ = query_in.shape
    group, taps_own = med_filter.shape
    width = short_filter.shape[2]
    size = 2 * block
    rows = block + ROW
    held_short = 3 * ROW
    parts = PARTS
    coarse = n_context // parts
    ahead, behind = halo_pairs(n_context)
    _, outer, both = groups_of(n_context, n_dp, parts)
    forward, inverse = transforms(block, width)
    tables = forward + [inverse]

    back = jnp.concatenate([x[:, block - ROW :] for x in (query_in, key_in, value_in)], axis=0)
    fore = jnp.concatenate([x[:, :ROW] for x in (query_in, key_in, value_in, grad_out)], axis=0)
    back = lax.ppermute(back, "context", ahead)
    fore = lax.ppermute(fore, "context", behind)

    short = short_filter.transpose(0, 2, 1).reshape(3 * width, group)
    short = jnp.pad(short, ((0, held_short - 3 * width), (0, 0)))
    taps = spread(short, n_context, "context")
    mine = lax.all_gather(
        med_filter.astype(BF).T, ("context", "dp"), axis_index_groups=both
    ).reshape(parts, block, group)
    h_all = spread(mine, coarse, "context", outer)

    whole = lambda x: pl.BlockSpec(x.shape, lambda *_: (0,) * x.ndim)
    pieces = []
    for first, count in CHUNKS:
        wide = count * group
        per = parts // count
        place = first // count
        cols = wide // LANES
        padded = pltpu.VMEM((cols, block + 2 * ROW, LANES), F32)
        at = lambda i, per=per, place=place: per * i + place
        tokens = pl.BlockSpec((1, block, wide), lambda i, at=at: (0, 0, at(i)))
        stack = lambda height, at=at: pl.BlockSpec((height, ROW, wide), lambda i: (0, 0, at(i)))
        filters = pl.BlockSpec((count, held_short, group), lambda i, at=at: (at(i), 0, 0))
        packed = lambda height: pl.BlockSpec((height, wide), lambda i: (0, i))
        u, dz = pl.pallas_call(
            functools.partial(make_products, block, width, cols),
            grid=(coarse,),
            in_specs=[tokens] * 4 + [stack(3), stack(4), filters],
            out_specs=[packed(block), packed(rows)],
            out_shape=[
                jax.ShapeDtypeStruct((block, coarse * wide), BF),
                jax.ShapeDtypeStruct((rows, coarse * wide), BF),
            ],
            scratch_shapes=[padded] * 3,
        )(query_in, key_in, value_in, grad_out, back, fore, taps)
        u_prev = lax.ppermute(u, "context", ahead)
        dz_next = lax.ppermute(dz, "context", behind)
        pieces.append((u_prev, dz_next))

    outs = None
    partials = []
    for index, (first, count) in enumerate(CHUNKS):
        wide = count * group
        per = parts // count
        place = first // count
        cols = wide // LANES
        at = lambda i, per=per, place=place: per * i + place
        tokens = pl.BlockSpec((1, block, wide), lambda i, at=at: (0, 0, at(i)))
        stack = lambda height, at=at: pl.BlockSpec((height, ROW, wide), lambda i: (0, 0, at(i)))
        filters = pl.BlockSpec((count, held_short, group), lambda i, at=at: (at(i), 0, 0))
        packed = lambda height: pl.BlockSpec((height, wide), lambda i: (0, i))
        taps_h = pl.BlockSpec((1, count, block, group), lambda i, place=place: (i, place, 0, 0))
        padded = pltpu.VMEM((cols, block + 2 * ROW, LANES), F32)
        shifted = pltpu.VMEM((cols, rows, LANES), F32)
        strip = lambda height: pltpu.VMEM((cols, height * ROW, LANES), F32)
        spectrum = pltpu.VMEM((count, size, group), F32)
        u_prev, dz_next = pieces[index]
        carried = [] if outs is None else list(outs)
        fixed = [query_in, key_in, value_in, grad_out, back, fore, taps, u_prev, dz_next]
        fixed += [h_all, *tables]
        *outs, partial = pl.pallas_call(
            functools.partial(mixer, block, width, count),
            grid=(coarse,),
            in_specs=[tokens] * 4
            + [stack(3), stack(4), filters, packed(block), packed(rows), taps_h]
            + [whole(x) for x in tables]
            + [pl.BlockSpec(memory_space=pl.ANY)] * len(carried),
            out_specs=[tokens] * 4
            + [pl.BlockSpec((1, count, block + held_short, group), lambda i: (i, 0, 0, 0))],
            out_shape=[jax.ShapeDtypeStruct(query_in.shape, BF)] * 4
            + [jax.ShapeDtypeStruct((coarse, count, block + held_short, group), BF)],
            scratch_shapes=[
                pltpu.VMEM((cols, held_short, ROW, LANES), F32),
                padded,
                padded,
                padded,
                shifted,
                shifted,
                shifted,
                pltpu.VMEM((cols, 3, rows, LANES), F32),
                strip(3),
                strip(2),
                strip(2),
                pltpu.VMEM((count, size, group), BF),
                pltpu.VMEM((count, block, group), BF),
                strip(1),
                strip(1),
                spectrum,
                spectrum,
                spectrum,
                spectrum,
            ],
            input_output_aliases={len(fixed) + k: k for k in range(len(carried))},
        )(*fixed, *carried)
        arrived = exchange(partial, "context", outer)
        partials.append(jnp.sum(arrived.astype(F32), axis=0))

    total = jnp.concatenate(partials, axis=0).astype(BF)
    med = total[:, :block].reshape(parts, n_dp, taps_own, group)
    extra = jnp.broadcast_to(total[:, None, block:], (parts, n_dp, held_short, group))
    sent = jnp.concatenate([med, extra], axis=2).reshape(parts * n_dp, taps_own + held_short, group)
    sent = exchange(sent, ("context", "dp"), both)
    final = jnp.sum(sent.astype(F32), axis=0)
    grad_med = final[:taps_own].T
    grad_short = final[taps_own : taps_own + 3 * width].reshape(3, width, group).transpose(0, 2, 1)
    return (*outs, grad_med, grad_short)


def solution(mesh):
    tokens = P("dp", "context", None)
    filters = (P("context", "dp"), P(None, "context", None))
    inner = functools.partial(per_device, mesh.shape["context"], mesh.shape["dp"])

    return jax.shard_map(
        inner,
        mesh=mesh,
        in_specs=(tokens,) * 4 + filters,
        out_specs=(tokens,) * 4 + filters,
        check_vma=False,
    )
```

```python
import functools

import jax
import jax.numpy as jnp
import numpy as np
from jax import lax
from jax.experimental import pallas as pl
from jax.experimental.pallas import tpu as pltpu
from jax.sharding import PartitionSpec as P


PARTS = 4
CHUNKS = ((0, 2), (2, 2))
BF = jnp.bfloat16
F32 = jnp.float32
LANES = 128
ROW = 8
TALL = 64


def phases(tokens, size):
    angle = 2.0 * np.pi * (np.arange(size // 2)[:, None] + 0.5) * tokens[None, :] / size
    return np.concatenate([np.cos(angle), np.sin(angle)], axis=0)


def split_host(table):
    high = table.astype(BF)
    low = (table - high.astype(np.float64)).astype(BF)
    return jnp.asarray(np.concatenate([high, low], axis=1))


def transforms(block, width):
    size = 2 * block
    reach = width - 1
    own = np.arange(block)
    behind = np.where(own < reach, own + block, own - block)
    ahead = own + block
    rows = np.arange(block + ROW)
    forward = [
        split_host(phases(np.concatenate([own, behind]), size)),
        split_host(phases(own, size)),
        split_host(phases(ahead, size)),
    ]
    inverse = split_host(phases(rows, size).T * (2.0 / size))
    return forward, inverse


def dot(a, b):
    return jnp.dot(a, b, preferred_element_type=F32)


def dot_twice(high_low, b):
    return dot(high_low, jnp.concatenate([b, b], axis=0))


def row_of(ref, index, col):
    per = ref.shape[2] // LANES
    return ref[col // per, pl.ds(index, 1), pl.ds(col % per * LANES, LANES)]


def load_padded(dst, own_ref, before, after, lanes, block):
    dst[pl.ds(0, ROW), :] = before
    dst[pl.ds(ROW, block), :] = own_ref[0, :, lanes].astype(F32)
    dst[pl.ds(ROW + block, ROW), :] = after


def causal(src, taps, first, width, col, rows):
    total = None
    for offset in range(width):
        term = row_of(taps, first + offset, col) * src[pl.ds(ROW - offset, rows), :]
        total = term if total is None else total + term
    return total


def make_products(block, width, cols, q, k, v, go, back, fore, taps, u_out, dz_out, x_q, x_k, x_v):
    for col in range(cols):
        lanes = pl.ds(col * LANES, LANES)
        for which, (src, dst) in enumerate(((q, x_q), (k, x_k), (v, x_v))):
            load_padded(
                dst.at[col],
                src,
                back[which, :, lanes].astype(F32),
                fore[which, :, lanes].astype(F32),
                lanes,
                block,
            )
        k_s = causal(x_k.at[col], taps, width, width, col, block)
        v_s = causal(x_v.at[col], taps, 2 * width, width, col, block)
        u_out[:, lanes] = (k_s * v_s).astype(BF)
        q_s = causal(x_q.at[col], taps, 0, width, col, block + ROW)
        dz_out[0:block, lanes] = (go[0, :, lanes].astype(F32) * q_s[0:block]).astype(BF)
        dz_out[block : block + ROW, lanes] = (
            fore[3, :, lanes].astype(F32) * q_s[block : block + ROW]
        ).astype(BF)


def mixer(block, width, subs, q, k, v, go, back, fore, taps, u_prev, dz_next, h_ref, *rest):
    rows = block + ROW
    half = block
    per = q.shape[2] // LANES // subs
    group = per * LANES
    t_window, t_own, t_ahead, t_inverse = rest[:4]
    outs = rest[len(rest) - 24 :]
    mixed, g_q, g_k, g_v, g_part, sums, x_q, x_k, x_v, s_q, s_k, s_v, g_pad = outs[:13]
    h_pad, h_flip, z_pad, window, dz_own, edge_u, edge_z, spec_u, spec_h, spec_d, spec_w = outs[13:]
    rank = lax.broadcasted_iota(jnp.int32, (ROW, LANES), 0)

    def gather_rows(sub, col):
        lanes = pl.ds(col * LANES, LANES)
        inside = pl.ds((col - sub * per) * LANES, LANES)
        for which, (src, dst) in enumerate(((q, x_q), (k, x_k), (v, x_v))):
            load_padded(
                dst.at[col],
                src,
                back[which, :, lanes].astype(F32),
                fore[which, :, lanes].astype(F32),
                lanes,
                block,
            )
        q_s = causal(x_q.at[col], taps, 0, width, col, rows)
        s_q[col] = q_s
        dz = (go[0, :, lanes].astype(F32) * q_s[0:block]).astype(BF)
        dz_own[sub, :, inside] = dz
        z_pad[col, 0:ROW, :] = jnp.zeros((ROW, LANES), F32)
        z_pad[col, ROW : 2 * ROW, :] = dz[0:ROW].astype(F32)
        k_s = causal(x_k.at[col], taps, width, width, col, rows)
        s_k[col] = k_s
        v_s = causal(x_v.at[col], taps, 2 * width, width, col, rows)
        s_v[col] = v_s
        u = (k_s * v_s).astype(BF)
        window[sub, 0:block, inside] = u[0:block]
        u_after = u[block:rows].astype(F32)
        first = u_prev[0 : 2 * ROW, lanes].astype(F32)
        u_before = first[0:ROW]
        patched = jnp.where(rank < width - 1, u_after, u_before)
        window[sub, block : block + 2 * ROW, inside] = jnp.concatenate(
            [patched, first[ROW : 2 * ROW]], axis=0
        ).astype(BF)
        window[sub, block + 2 * ROW : 2 * block, inside] = u_prev[2 * ROW : block, lanes]
        edge_u[col] = u_before + u_after
        edge_z[col] = dz_next[block : block + ROW, lanes].astype(F32) + dz[0:ROW].astype(F32)
        h_pad[col, 0 : 2 * ROW, :] = h_ref[0, sub, block - 2 * ROW : block, inside].astype(F32)
        h_pad[col, 2 * ROW : 3 * ROW, :] = jnp.zeros((ROW, LANES), F32)
        h_flip[col, 0:ROW, :] = jnp.zeros((ROW, LANES), F32)
        for place in range(width - 2):
            h_flip[col, ROW + place : ROW + place + 1, :] = h_pad[
                col, 2 * ROW - 1 - place : 2 * ROW - place, :
            ]

    def spectra(sub):
        lanes = pl.ds(sub * group, group)
        x = window[sub]
        spec_u[sub] = dot_twice(t_window[...], x)
        h = h_ref[0, sub]
        spec_h[sub] = dot_twice(t_own[...], h)
        d = dz_own[sub]
        spec_d[sub] = dot_twice(t_own[...], d)
        a = dz_next[0:block, lanes]
        spec_w[sub] = spec_d[sub] + dot_twice(t_ahead[...], a)

    def inverse(cos_part, sin_part, count):
        high = jnp.concatenate([cos_part.astype(BF), sin_part.astype(BF)], axis=0)
        return dot_twice(t_inverse[0:count, :], high)

    def times(sub, lanes):
        uc, us = spec_u[sub, 0:half, lanes], spec_u[sub, half:, lanes]
        hc, hs = spec_h[sub, 0:half, lanes], spec_h[sub, half:, lanes]
        z = inverse(uc * hc - us * hs, uc * hs + us * hc, rows)
        wc, ws = spec_w[sub, 0:half, lanes], spec_w[sub, half:, lanes]
        du = inverse(wc * hc + ws * hs, ws * hc - wc * hs, rows)
        dc, ds = spec_d[sub, 0:half, lanes], spec_d[sub, half:, lanes]
        gm = inverse(dc * uc + ds * us, ds * uc - dc * us, block)
        return z, du, gm

    def finish(sub, col, z, du, gm):
        lanes = pl.ds(col * LANES, LANES)
        inside = pl.ds((col - sub * per) * LANES, LANES)
        z_fix = jnp.zeros((ROW, LANES), F32)
        g_fix = jnp.zeros((ROW, LANES), F32)
        for place in range(1, width - 1):
            held = edge_u[col, place : place + 1, :]
            z_fix = z_fix + held * h_pad[col, pl.ds(2 * ROW - place, ROW), :]
            g_fix = g_fix + held * z_pad[col, pl.ds(place, ROW), :]
        du_fix = jnp.zeros((ROW, LANES), F32)
        for place in range(width - 2):
            held = edge_z[col, place : place + 1, :]
            du_fix = du_fix + held * h_flip[col, pl.ds(ROW - 1 - place, ROW), :]
        z = jnp.concatenate([z[0:ROW] + z_fix, z[ROW:]], axis=0)
        du = jnp.concatenate([du[0:block], du[block:] + du_fix], axis=0)
        gm = jnp.concatenate([gm[0 : block - ROW], gm[block - ROW : block] + g_fix], axis=0)
        g_part[0, sub, 0:block, inside] = gm.astype(BF)
        mixed[0, :, lanes] = (s_q[col, 0:block, :] * z[0:block]).astype(BF)
        g_pad[col, 0, 0:block, :] = go[0, :, lanes].astype(F32) * z[0:block]
        g_pad[col, 0, block:rows, :] = fore[3, :, lanes].astype(F32) * z[block:rows]
        g_pad[col, 1] = du * s_v[col]
        g_pad[col, 2] = du * s_k[col]
        for which, (src, out) in enumerate(((x_q, g_q), (x_k, g_k), (x_v, g_v))):
            for start in range(0, block, TALL):
                values = src[col, ROW + start : ROW + start + TALL, :]
                total = None
                for offset in range(width):
                    moved = g_pad[col, which, pl.ds(start + offset, TALL), :]
                    term = row_of(taps, which * width + offset, col) * moved
                    total = term if total is None else total + term
                    weight = values * moved
                    held = weight[0:ROW]
                    for r in range(ROW, TALL, ROW):
                        held = held + weight[r : r + ROW]
                    place = which * width + offset
                    if start == 0:
                        sums[col, place] = held
                    else:
                        sums[col, place] = sums[col, place] + held
                out[0, start : start + TALL, lanes] = total.astype(BF)
        g_part[0, sub, block : block + 3 * ROW, inside] = jnp.sum(sums[col], axis=1).astype(BF)

    for sub in range(subs):
        for col in range(sub * per, (sub + 1) * per):
            gather_rows(sub, col)
        spectra(sub)
    for sub in range(subs):
        found = times(sub, pl.ds(0, group))
        for col in range(sub * per, (sub + 1) * per):
            lo = (col - sub * per) * LANES
            finish(sub, col, *(x[:, lo : lo + LANES] for x in found))


def halo_pairs(count):
    return [(i, i + 1) for i in range(count - 1)], [(i + 1, i) for i in range(count - 1)]


def groups_of(n_context, n_dp, fine):
    coarse = n_context // fine
    inner = [[c * fine + f for f in range(fine)] for c in range(coarse)]
    outer = [[c * fine + f for c in range(coarse)] for f in range(fine)]
    both = [
        [(c * fine + f) * n_dp + d for f in range(fine) for d in range(n_dp)] for c in range(coarse)
    ]
    return inner, outer, both


def exchange(x, axes, groups=None):
    return lax.all_to_all(x, axes, 0, 0, axis_index_groups=groups)


def spread(x, count, axes, groups=None):
    return exchange(jnp.broadcast_to(x, (count,) + x.shape), axes, groups)


def per_device(n_context, n_dp, query_in, key_in, value_in, grad_out, med_filter, short_filter):
    _, block, _ = query_in.shape
    group, taps_own = med_filter.shape
    width = short_filter.shape[2]
    size = 2 * block
    rows = block + ROW
    held_short = 3 * ROW
    parts = PARTS
    coarse = n_context // parts
    ahead, behind = halo_pairs(n_context)
    inner, outer, both = groups_of(n_context, n_dp, parts)
    forward, inverse = transforms(block, width)
    tables = forward + [inverse]

    back = jnp.concatenate([x[:, block - ROW :] for x in (query_in, key_in, value_in)], axis=0)
    fore = jnp.concatenate([x[:, :ROW] for x in (query_in, key_in, value_in, grad_out)], axis=0)
    back = lax.ppermute(back, "context", ahead)
    fore = lax.ppermute(fore, "context", behind)

    short = short_filter.transpose(0, 2, 1).reshape(3 * width, group)
    short = jnp.pad(short, ((0, held_short - 3 * width), (0, 0)))
    taps = spread(short, n_context, "context")
    mine = lax.all_gather(med_filter.astype(BF).T, "dp", axis=0, tiled=True)
    mine = spread(mine, parts, "context", inner)
    h_all = []
    for first, count in CHUNKS:
        h_all.append(spread(mine[first : first + count], coarse, "context", outer))

    whole = lambda x: pl.BlockSpec(x.shape, lambda *_: (0,) * x.ndim)
    pieces = []
    for first, count in CHUNKS:
        wide = count * group
        per = parts // count
        place = first // count
        cols = wide // LANES
        padded = pltpu.VMEM((cols, block + 2 * ROW, LANES), F32)
        at = lambda i, per=per, place=place: per * i + place
        tokens = pl.BlockSpec((1, block, wide), lambda i, at=at: (0, 0, at(i)))
        stack = lambda height, at=at: pl.BlockSpec((height, ROW, wide), lambda i: (0, 0, at(i)))
        filters = pl.BlockSpec((count, held_short, group), lambda i, at=at: (at(i), 0, 0))
        packed = lambda height: pl.BlockSpec((height, wide), lambda i: (0, i))
        u, dz = pl.pallas_call(
            functools.partial(make_products, block, width, cols),
            grid=(coarse,),
            in_specs=[tokens] * 4 + [stack(3), stack(4), filters],
            out_specs=[packed(block), packed(rows)],
            out_shape=[
                jax.ShapeDtypeStruct((block, coarse * wide), BF),
                jax.ShapeDtypeStruct((rows, coarse * wide), BF),
            ],
            scratch_shapes=[padded] * 3,
        )(query_in, key_in, value_in, grad_out, back, fore, taps)
        u_prev = lax.ppermute(u, "context", ahead)
        dz_next = lax.ppermute(dz, "context", behind)
        pieces.append((u_prev, dz_next))

    outs = None
    partials = []
    for index, (first, count) in enumerate(CHUNKS):
        wide = count * group
        per = parts // count
        place = first // count
        cols = wide // LANES
        at = lambda i, per=per, place=place: per * i + place
        tokens = pl.BlockSpec((1, block, wide), lambda i, at=at: (0, 0, at(i)))
        stack = lambda height, at=at: pl.BlockSpec((height, ROW, wide), lambda i: (0, 0, at(i)))
        filters = pl.BlockSpec((count, held_short, group), lambda i, at=at: (at(i), 0, 0))
        packed = lambda height: pl.BlockSpec((height, wide), lambda i: (0, i))
        taps_h = pl.BlockSpec((1, count, block, group), lambda i: (i, 0, 0, 0))
        padded = pltpu.VMEM((cols, block + 2 * ROW, LANES), F32)
        shifted = pltpu.VMEM((cols, rows, LANES), F32)
        strip = lambda height: pltpu.VMEM((cols, height * ROW, LANES), F32)
        spectrum = pltpu.VMEM((count, size, group), F32)
        u_prev, dz_next = pieces[index]
        carried = [] if outs is None else list(outs)
        fixed = [query_in, key_in, value_in, grad_out, back, fore, taps, u_prev, dz_next]
        fixed += [h_all[index], *tables]
        *outs, partial = pl.pallas_call(
            functools.partial(mixer, block, width, count),
            grid=(coarse,),
            in_specs=[tokens] * 4
            + [stack(3), stack(4), filters, packed(block), packed(rows), taps_h]
            + [whole(x) for x in tables]
            + [pl.BlockSpec(memory_space=pl.ANY)] * len(carried),
            out_specs=[tokens] * 4
            + [pl.BlockSpec((1, count, block + held_short, group), lambda i: (i, 0, 0, 0))],
            out_shape=[jax.ShapeDtypeStruct(query_in.shape, BF)] * 4
            + [jax.ShapeDtypeStruct((coarse, count, block + held_short, group), BF)],
            scratch_shapes=[
                pltpu.VMEM((cols, held_short, ROW, LANES), F32),
                padded,
                padded,
                padded,
                shifted,
                shifted,
                shifted,
                pltpu.VMEM((cols, 3, rows, LANES), F32),
                strip(3),
                strip(2),
                strip(2),
                pltpu.VMEM((count, size, group), BF),
                pltpu.VMEM((count, block, group), BF),
                strip(1),
                strip(1),
                spectrum,
                spectrum,
                spectrum,
                spectrum,
            ],
            input_output_aliases={len(fixed) + k: k for k in range(len(carried))},
        )(*fixed, *carried)
        arrived = exchange(partial, "context", outer)
        partials.append(jnp.sum(arrived.astype(F32), axis=0))

    total = jnp.concatenate(partials, axis=0).astype(BF)
    med = total[:, :block].reshape(parts, n_dp, taps_own, group)
    extra = jnp.broadcast_to(total[:, None, block:], (parts, n_dp, held_short, group))
    sent = jnp.concatenate([med, extra], axis=2).reshape(parts * n_dp, taps_own + held_short, group)
    sent = exchange(sent, ("context", "dp"), both)
    final = jnp.sum(sent.astype(F32), axis=0)
    grad_med = final[:taps_own].T
    grad_short = final[taps_own : taps_own + 3 * width].reshape(3, width, group).transpose(0, 2, 1)
    return (*outs, grad_med, grad_short)


def solution(mesh):
    tokens = P("dp", "context", None)
    filters = (P("context", "dp"), P(None, "context", None))
    inner = functools.partial(per_device, mesh.shape["context"], mesh.shape["dp"])

    return jax.shard_map(
        inner,
        mesh=mesh,
        in_specs=(tokens,) * 4 + filters,
        out_specs=(tokens,) * 4 + filters,
        check_vma=False,
    )
```

```python
import functools

import jax
import jax.numpy as jnp
import numpy as np
from jax import lax
from jax.experimental import pallas as pl
from jax.experimental.pallas import tpu as pltpu
from jax.sharding import PartitionSpec as P


PARTS = 4
CHUNKS = ((0, 2), (2, 2))
BF = jnp.bfloat16
F32 = jnp.float32
LANES = 128
ROW = 8
TALL = 64


def phases(tokens, size):
    angle = 2.0 * np.pi * (np.arange(size // 2)[:, None] + 0.5) * tokens[None, :] / size
    return np.concatenate([np.cos(angle), np.sin(angle)], axis=0)


def split_host(table):
    high = table.astype(BF)
    low = (table - high.astype(np.float64)).astype(BF)
    return jnp.asarray(np.concatenate([high, low], axis=1))


def transforms(block, width):
    size = 2 * block
    reach = width - 1
    own = np.arange(block)
    behind = np.where(own < reach, own + block, own - block)
    ahead = own + block
    rows = np.arange(block + ROW)
    forward = [
        split_host(phases(np.concatenate([own, behind]), size)),
        split_host(phases(own, size)),
        split_host(phases(ahead, size)),
    ]
    inverse = split_host(phases(rows, size).T * (2.0 / size))
    return forward, inverse


def dot(a, b):
    return jnp.dot(a, b, preferred_element_type=F32)


def dot_twice(high_low, b):
    return dot(high_low, jnp.concatenate([b, b], axis=0))


def row_of(ref, index, col):
    per = ref.shape[2] // LANES
    return ref[col // per, pl.ds(index, 1), pl.ds(col % per * LANES, LANES)]


def load_padded(dst, own_ref, before, after, lanes, block):
    dst[pl.ds(0, ROW), :] = before
    dst[pl.ds(ROW, block), :] = own_ref[0, :, lanes].astype(F32)
    dst[pl.ds(ROW + block, ROW), :] = after


def causal(src, taps, first, width, col, rows):
    total = None
    for offset in range(width):
        term = row_of(taps, first + offset, col) * src[pl.ds(ROW - offset, rows), :]
        total = term if total is None else total + term
    return total


def make_products(block, width, cols, q, k, v, go, back, fore, taps, u_out, dz_out, x_q, x_k, x_v):
    for col in range(cols):
        lanes = pl.ds(col * LANES, LANES)
        for which, (src, dst) in enumerate(((q, x_q), (k, x_k), (v, x_v))):
            load_padded(
                dst.at[col],
                src,
                back[which, :, lanes].astype(F32),
                fore[which, :, lanes].astype(F32),
                lanes,
                block,
            )
        k_s = causal(x_k.at[col], taps, width, width, col, block)
        v_s = causal(x_v.at[col], taps, 2 * width, width, col, block)
        u_out[:, lanes] = (k_s * v_s).astype(BF)
        q_s = causal(x_q.at[col], taps, 0, width, col, block + ROW)
        dz_out[0:block, lanes] = (go[0, :, lanes].astype(F32) * q_s[0:block]).astype(BF)
        dz_out[block : block + ROW, lanes] = (
            fore[3, :, lanes].astype(F32) * q_s[block : block + ROW]
        ).astype(BF)


def mixer(block, width, subs, q, k, v, go, back, fore, taps, u_prev, dz_next, h_mine, h_other, h_last, *rest):
    rows = block + ROW
    half = block
    per = q.shape[2] // LANES // subs
    group = per * LANES
    t_window, t_own, t_ahead, t_inverse, t_taps = rest[:5]
    outs = rest[len(rest) - 24 :]
    mixed, g_q, g_k, g_v, g_part, sums, x_q, x_k, x_v, s_q, s_k, s_v, g_pad = outs[:13]
    h_pad, h_flip, z_pad, window, dz_own, edge_u, edge_z, spec_u, spec_h, spec_d, spec_w = outs[13:]
    rank = lax.broadcasted_iota(jnp.int32, (ROW, LANES), 0)

    def gather_rows(sub, col):
        lanes = pl.ds(col * LANES, LANES)
        inside = pl.ds((col - sub * per) * LANES, LANES)
        for which, (src, dst) in enumerate(((q, x_q), (k, x_k), (v, x_v))):
            load_padded(
                dst.at[col],
                src,
                back[which, :, lanes].astype(F32),
                fore[which, :, lanes].astype(F32),
                lanes,
                block,
            )
        q_s = causal(x_q.at[col], taps, 0, width, col, rows)
        s_q[col] = q_s
        dz = (go[0, :, lanes].astype(F32) * q_s[0:block]).astype(BF)
        dz_own[sub, :, inside] = dz
        z_pad[col, 0:ROW, :] = jnp.zeros((ROW, LANES), F32)
        z_pad[col, ROW : 2 * ROW, :] = dz[0:ROW].astype(F32)
        k_s = causal(x_k.at[col], taps, width, width, col, rows)
        s_k[col] = k_s
        v_s = causal(x_v.at[col], taps, 2 * width, width, col, rows)
        s_v[col] = v_s
        u = (k_s * v_s).astype(BF)
        window[sub, 0:block, inside] = u[0:block]
        u_after = u[block:rows].astype(F32)
        first = u_prev[0 : 2 * ROW, lanes].astype(F32)
        u_before = first[0:ROW]
        patched = jnp.where(rank < width - 1, u_after, u_before)
        window[sub, block : block + 2 * ROW, inside] = jnp.concatenate(
            [patched, first[ROW : 2 * ROW]], axis=0
        ).astype(BF)
        window[sub, block + 2 * ROW : 2 * block, inside] = u_prev[2 * ROW : block, lanes]
        edge_u[col] = u_before + u_after
        edge_z[col] = dz_next[block : block + ROW, lanes].astype(F32) + dz[0:ROW].astype(F32)
        h_pad[col, 0 : 2 * ROW, :] = h_last[0, sub, :, inside].astype(F32)
        h_pad[col, 2 * ROW : 3 * ROW, :] = jnp.zeros((ROW, LANES), F32)
        h_flip[col, 0:ROW, :] = jnp.zeros((ROW, LANES), F32)
        for place in range(width - 2):
            h_flip[col, ROW + place : ROW + place + 1, :] = h_pad[
                col, 2 * ROW - 1 - place : 2 * ROW - place, :
            ]

    def spectra(sub):
        lanes = pl.ds(sub * group, group)
        x = window[sub]
        spec_u[sub] = dot_twice(t_window[...], x)
        h = jnp.concatenate([h_mine[0, sub], h_other[0, sub]], axis=0)
        spec_h[sub] = dot_twice(t_taps[...], h)
        d = dz_own[sub]
        spec_d[sub] = dot_twice(t_own[...], d)
        a = dz_next[0:block, lanes]
        spec_w[sub] = spec_d[sub] + dot_twice(t_ahead[...], a)

    def inverse(cos_part, sin_part, count):
        high = jnp.concatenate([cos_part.astype(BF), sin_part.astype(BF)], axis=0)
        return dot_twice(t_inverse[0:count, :], high)

    def times(sub, lanes):
        uc, us = spec_u[sub, 0:half, lanes], spec_u[sub, half:, lanes]
        hc, hs = spec_h[sub, 0:half, lanes], spec_h[sub, half:, lanes]
        z = inverse(uc * hc - us * hs, uc * hs + us * hc, rows)
        wc, ws = spec_w[sub, 0:half, lanes], spec_w[sub, half:, lanes]
        du = inverse(wc * hc + ws * hs, ws * hc - wc * hs, rows)
        dc, ds = spec_d[sub, 0:half, lanes], spec_d[sub, half:, lanes]
        gm = inverse(dc * uc + ds * us, ds * uc - dc * us, block)
        return z, du, gm

    def finish(sub, col, z, du, gm):
        lanes = pl.ds(col * LANES, LANES)
        inside = pl.ds((col - sub * per) * LANES, LANES)
        z_fix = jnp.zeros((ROW, LANES), F32)
        g_fix = jnp.zeros((ROW, LANES), F32)
        for place in range(1, width - 1):
            held = edge_u[col, place : place + 1, :]
            z_fix = z_fix + held * h_pad[col, pl.ds(2 * ROW - place, ROW), :]
            g_fix = g_fix + held * z_pad[col, pl.ds(place, ROW), :]
        du_fix = jnp.zeros((ROW, LANES), F32)
        for place in range(width - 2):
            held = edge_z[col, place : place + 1, :]
            du_fix = du_fix + held * h_flip[col, pl.ds(ROW - 1 - place, ROW), :]
        z = jnp.concatenate([z[0:ROW] + z_fix, z[ROW:]], axis=0)
        du = jnp.concatenate([du[0:block], du[block:] + du_fix], axis=0)
        gm = jnp.concatenate([gm[0 : block - ROW], gm[block - ROW : block] + g_fix], axis=0)
        g_part[0, sub, 0:block, inside] = gm.astype(BF)
        mixed[0, :, lanes] = (s_q[col, 0:block, :] * z[0:block]).astype(BF)
        g_pad[col, 0, 0:block, :] = go[0, :, lanes].astype(F32) * z[0:block]
        g_pad[col, 0, block:rows, :] = fore[3, :, lanes].astype(F32) * z[block:rows]
        g_pad[col, 1] = du * s_v[col]
        g_pad[col, 2] = du * s_k[col]
        for which, (src, out) in enumerate(((x_q, g_q), (x_k, g_k), (x_v, g_v))):
            for start in range(0, block, TALL):
                values = src[col, ROW + start : ROW + start + TALL, :]
                total = None
                for offset in range(width):
                    moved = g_pad[col, which, pl.ds(start + offset, TALL), :]
                    term = row_of(taps, which * width + offset, col) * moved
                    total = term if total is None else total + term
                    weight = values * moved
                    held = weight[0:ROW]
                    for r in range(ROW, TALL, ROW):
                        held = held + weight[r : r + ROW]
                    place = which * width + offset
                    if start == 0:
                        sums[col, place] = held
                    else:
                        sums[col, place] = sums[col, place] + held
                out[0, start : start + TALL, lanes] = total.astype(BF)
        g_part[0, sub, block : block + 3 * ROW, inside] = jnp.sum(sums[col], axis=1).astype(BF)

    for sub in range(subs):
        for col in range(sub * per, (sub + 1) * per):
            gather_rows(sub, col)
        spectra(sub)
    for sub in range(subs):
        found = times(sub, pl.ds(0, group))
        for col in range(sub * per, (sub + 1) * per):
            lo = (col - sub * per) * LANES
            finish(sub, col, *(x[:, lo : lo + LANES] for x in found))


def halo_pairs(count):
    return [(i, i + 1) for i in range(count - 1)], [(i + 1, i) for i in range(count - 1)]


def groups_of(n_context, n_dp, fine):
    coarse = n_context // fine
    inner = [[c * fine + f for f in range(fine)] for c in range(coarse)]
    outer = [[c * fine + f for c in range(coarse)] for f in range(fine)]
    both = [
        [(c * fine + f) * n_dp + d for f in range(fine) for d in range(n_dp)] for c in range(coarse)
    ]
    return inner, outer, both


def exchange(x, axes, groups=None):
    return lax.all_to_all(x, axes, 0, 0, axis_index_groups=groups)


def spread(x, count, axes, groups=None):
    return exchange(jnp.broadcast_to(x, (count,) + x.shape), axes, groups)


def per_device(n_context, n_dp, query_in, key_in, value_in, grad_out, med_filter, short_filter):
    _, block, _ = query_in.shape
    group, taps_own = med_filter.shape
    width = short_filter.shape[2]
    size = 2 * block
    rows = block + ROW
    held_short = 3 * ROW
    parts = PARTS
    coarse = n_context // parts
    ahead, behind = halo_pairs(n_context)
    inner, outer, both = groups_of(n_context, n_dp, parts)
    forward, inverse = transforms(block, width)
    tables = forward + [inverse]

    back = jnp.concatenate([x[:, block - ROW :] for x in (query_in, key_in, value_in)], axis=0)
    fore = jnp.concatenate([x[:, :ROW] for x in (query_in, key_in, value_in, grad_out)], axis=0)
    back = lax.ppermute(back, "context", ahead)
    fore = lax.ppermute(fore, "context", behind)

    short = short_filter.transpose(0, 2, 1).reshape(3 * width, group)
    short = jnp.pad(short, ((0, held_short - 3 * width), (0, 0)))
    taps = spread(short, n_context, "context")
    parity = lax.axis_index("dp") & 1
    half = block // 2
    mine = lax.all_gather(
        med_filter.astype(BF).T,
        "dp",
        axis=0,
        tiled=True,
        axis_index_groups=[list(range(core, n_dp, 2)) for core in range(2)],
    )
    mine = spread(mine, parts, "context", inner)
    h_mine = spread(mine, coarse, "context", outer)
    h_other = lax.ppermute(h_mine, "dp", [(i, i + 1 - 2 * (i % 2)) for i in range(n_dp)])
    h_last = jnp.where(parity == 1, h_mine, h_other)[:, :, half - 2 * ROW :]
    own_taps = [
        np.concatenate([np.arange(d * taps_own, (d + 1) * taps_own) for d in range(core, n_dp, 2)])
        for core in range(2)
    ]
    choices = [split_host(phases(np.concatenate([own_taps[c], own_taps[1 - c]]), size)) for c in (0, 1)]
    tables.append(jnp.where(parity == 0, choices[0], choices[1]))

    whole = lambda x: pl.BlockSpec(x.shape, lambda *_: (0,) * x.ndim)
    pieces = []
    for first, count in CHUNKS:
        wide = count * group
        per = parts // count
        place = first // count
        cols = wide // LANES
        padded = pltpu.VMEM((cols, block + 2 * ROW, LANES), F32)
        at = lambda i, per=per, place=place: per * i + place
        tokens = pl.BlockSpec((1, block, wide), lambda i, at=at: (0, 0, at(i)))
        stack = lambda height, at=at: pl.BlockSpec((height, ROW, wide), lambda i: (0, 0, at(i)))
        filters = pl.BlockSpec((count, held_short, group), lambda i, at=at: (at(i), 0, 0))
        packed = lambda height: pl.BlockSpec((height, wide), lambda i: (0, i))
        u, dz = pl.pallas_call(
            functools.partial(make_products, block, width, cols),
            grid=(coarse,),
            in_specs=[tokens] * 4 + [stack(3), stack(4), filters],
            out_specs=[packed(block), packed(rows)],
            out_shape=[
                jax.ShapeDtypeStruct((block, coarse * wide), BF),
                jax.ShapeDtypeStruct((rows, coarse * wide), BF),
            ],
            scratch_shapes=[padded] * 3,
        )(query_in, key_in, value_in, grad_out, back, fore, taps)
        u_prev = lax.ppermute(u, "context", ahead)
        dz_next = lax.ppermute(dz, "context", behind)
        pieces.append((u_prev, dz_next))

    outs = None
    partials = []
    for index, (first, count) in enumerate(CHUNKS):
        wide = count * group
        per = parts // count
        place = first // count
        cols = wide // LANES
        at = lambda i, per=per, place=place: per * i + place
        tokens = pl.BlockSpec((1, block, wide), lambda i, at=at: (0, 0, at(i)))
        stack = lambda height, at=at: pl.BlockSpec((height, ROW, wide), lambda i: (0, 0, at(i)))
        filters = pl.BlockSpec((count, held_short, group), lambda i, at=at: (at(i), 0, 0))
        packed = lambda height: pl.BlockSpec((height, wide), lambda i: (0, i))
        taps_h = lambda height, place=place: pl.BlockSpec(
            (1, count, height, group), lambda i: (i, place, 0, 0)
        )
        padded = pltpu.VMEM((cols, block + 2 * ROW, LANES), F32)
        shifted = pltpu.VMEM((cols, rows, LANES), F32)
        strip = lambda height: pltpu.VMEM((cols, height * ROW, LANES), F32)
        spectrum = pltpu.VMEM((count, size, group), F32)
        u_prev, dz_next = pieces[index]
        carried = [] if outs is None else list(outs)
        fixed = [query_in, key_in, value_in, grad_out, back, fore, taps, u_prev, dz_next]
        fixed += [h_mine, h_other, h_last, *tables]
        *outs, partial = pl.pallas_call(
            functools.partial(mixer, block, width, count),
            grid=(coarse,),
            in_specs=[tokens] * 4
            + [stack(3), stack(4), filters, packed(block), packed(rows)]
            + [taps_h(half), taps_h(half), taps_h(2 * ROW)]
            + [whole(x) for x in tables]
            + [pl.BlockSpec(memory_space=pl.ANY)] * len(carried),
            out_specs=[tokens] * 4
            + [pl.BlockSpec((1, count, block + held_short, group), lambda i: (i, 0, 0, 0))],
            out_shape=[jax.ShapeDtypeStruct(query_in.shape, BF)] * 4
            + [jax.ShapeDtypeStruct((coarse, count, block + held_short, group), BF)],
            scratch_shapes=[
                pltpu.VMEM((cols, held_short, ROW, LANES), F32),
                padded,
                padded,
                padded,
                shifted,
                shifted,
                shifted,
                pltpu.VMEM((cols, 3, rows, LANES), F32),
                strip(3),
                strip(2),
                strip(2),
                pltpu.VMEM((count, size, group), BF),
                pltpu.VMEM((count, block, group), BF),
                strip(1),
                strip(1),
                spectrum,
                spectrum,
                spectrum,
                spectrum,
            ],
            input_output_aliases={len(fixed) + k: k for k in range(len(carried))},
        )(*fixed, *carried)
        arrived = exchange(partial, "context", outer)
        partials.append(jnp.sum(arrived.astype(F32), axis=0))

    total = jnp.concatenate(partials, axis=0).astype(BF)
    med = total[:, :block].reshape(parts, n_dp, taps_own, group)
    extra = jnp.broadcast_to(total[:, None, block:], (parts, n_dp, held_short, group))
    sent = jnp.concatenate([med, extra], axis=2).reshape(parts * n_dp, taps_own + held_short, group)
    sent = exchange(sent, ("context", "dp"), both)
    final = jnp.sum(sent.astype(F32), axis=0)
    grad_med = final[:taps_own].T
    grad_short = final[taps_own : taps_own + 3 * width].reshape(3, width, group).transpose(0, 2, 1)
    return (*outs, grad_med, grad_short)


def solution(mesh):
    tokens = P("dp", "context", None)
    filters = (P("context", "dp"), P(None, "context", None))
    inner = functools.partial(per_device, mesh.shape["context"], mesh.shape["dp"])

    return jax.shard_map(
        inner,
        mesh=mesh,
        in_specs=(tokens,) * 4 + filters,
        out_specs=(tokens,) * 4 + filters,
        check_vma=False,
    )
```
